128 devices in a mesh: lat: 8 (over z, core), lonr: 16 (over x, y).
Axes of the slice: x: 4, y: 4, z: 4, core: 2. Of those that a mesh axis runs over, the one named last changes fastest.
Arguments:
- entropy: float32 [40, 1024, 2048], P(None, 'lat', 'lonr'), may hold values from 5 to 6
- zonal_flux: float32 [40, 1024, 2048], P(None, 'lat', 'lonr'), may hold values from 1.5 to 3.5
- meridional_flux: float32 [40, 1024, 2048], P(None, 'lat', 'lonr'), may hold values from -0.6 to 0.6
- start_entropy: float32 [40, 1024, 2048], P(None, 'lat', 'lonr'), may hold values from -6 to 6
- start_pressure: float32 [40, 1024, 2048], P(None, 'lat', 'lonr'), may hold values from -6 to 6
- order_slot: int32 [768], replicated, may hold values from 0 to 767, as said below
Outputs:
- new_entropy: float32 [40, 1024, 2048], P(None, 'lat', 'lonr')
- new_pressure: float32 [40, 1024, 2048], P(None, 'lat', 'lonr')
- spectrum: float32 [768, 64, 2, 768], P(('lat', 'lonr'))
The draws below stay inside these ranges and needn't reach their ends.
Inputs may be any that keep to these rules, and one draw needn't show every extreme that they name: order_slot is a permutation of the orders; slots 2k and 2k + 1 hold two orders whose sum is 767.
All inputs are finite; a program needn't handle non-finite values.
Results may differ from the reference program's by a relative error of at most 0.0058.
Values may be sent and summed in bfloat16 or wider, within the bound.
No kernel may reach another device: no remote copies, remote signals or barrier semaphores. Data moves between devices by JAX's collectives and lax.ppermute only.
A program may use at most 192 MiB of HBM per device.

```python
import math
import jax
import jax.numpy as jnp
from jax import lax

NLAT = 1024
NLON = 2048
ORDERS = 768
FLEV = 32
LEV = 40
ITEMS = 64
N_LAT = 8
N_LONR = 16


def draw_order_slot(key, part):
    half_count = ORDERS // 2
    low_order = jax.random.permutation(key, half_count).astype(jnp.int32)
    flip_bits = jax.random.randint(jax.random.fold_in(key, 7), (half_count,), 0, 2).astype(jnp.int32)
    first_order = jnp.where(flip_bits == 1, ORDERS - 1 - low_order, low_order)
    return jnp.stack((first_order, ORDERS - 1 - first_order), axis=1).reshape(ORDERS).astype(jnp.int32)


def profile_angles(key):
    rate_key, phase_key = jax.random.split(key)
    rate = jax.random.uniform(rate_key, (LEV, 1, 1), jnp.float32, 0.5, 3.0)
    phase = jax.random.uniform(phase_key, (LEV, 1, 1), jnp.float32, -math.pi, math.pi)
    colatitude = math.pi * (jnp.arange(NLAT, dtype=jnp.float32) + 0.5) / NLAT
    return rate * colatitude[None, :, None] + phase


def draw_entropy(key, part):
    shape_key, along_key, rough_key = jax.random.split(jax.random.fold_in(key, 11), 3)
    angles = profile_angles(shape_key)
    profile = 1.0 + 0.5 * jnp.cos(angles)
    along = jax.random.truncated_normal(along_key, -4.0, 4.0, (LEV, 1, NLON), jnp.float32)
    rough = jax.random.truncated_normal(rough_key, -4.0, 4.0, (LEV, NLAT, NLON), jnp.float32)
    field = 5.5 + 0.06 * profile * along + 0.03 * rough
    return field.astype(jnp.float32)


def draw_zonal_flux(key, part):
    shape_key, along_key, rough_key = jax.random.split(jax.random.fold_in(key, 23), 3)
    angles = profile_angles(shape_key)
    profile = 1.0 + 0.5 * jnp.cos(angles)
    along = jax.random.truncated_normal(along_key, -4.0, 4.0, (LEV, 1, NLON), jnp.float32)
    rough = jax.random.truncated_normal(rough_key, -4.0, 4.0, (LEV, NLAT, NLON), jnp.float32)
    field = 2.5 + 0.1 * profile * along + 0.03 * rough
    return field.astype(jnp.float32)


def steps_of(stream_key, extent, shards, low, largest):
    loudness = 1.0
    for axis_at, parts in shards:
        draws = jax.random.uniform(jax.random.fold_in(jax.random.fold_in(stream_key, 6), axis_at), (parts,), jnp.float32, low / len(shards), largest / len(shards))
        loudness = loudness * jnp.repeat(jnp.exp(draws), extent[axis_at] // parts).reshape((-1,) + (1,) * (len(extent) - 1 - axis_at))
    return loudness


def noise(stream_key, shape, scale, most, cuts=(), kind=jnp.bfloat16):
    values = scale * jax.random.normal(stream_key, shape, jnp.float32)
    if cuts:
        values = values * steps_of(stream_key, shape, cuts, -0.22, 0.18)
    return jnp.clip(values, -most, most).astype(kind)


def setup_inputs(seed: int = 0) -> dict:
    splits = jax.random.split(jax.random.key(seed), 7)
    return {
        "entropy": draw_entropy(jax.random.fold_in(splits[6], 71), 0),
        "zonal_flux": draw_zonal_flux(jax.random.fold_in(splits[6], 71), 0),
        "meridional_flux": noise(splits[2], (LEV, NLAT, NLON), 0.1, 0.6, ((1, 8), (2, 16)), jnp.float32),
        "start_entropy": noise(splits[3], (LEV, NLAT, NLON), 1.0, 6.0, ((1, 8), (2, 16)), jnp.float32),
        "start_pressure": noise(splits[4], (LEV, NLAT, NLON), 1.0, 6.0, ((1, 8), (2, 16)), jnp.float32),
        "order_slot": draw_order_slot(jax.random.fold_in(splits[6], 71), 0),
    }


section_weight = 0.5
sound_factor = 0.3
gamma_three_halves = 0.5 * math.log(math.pi) - math.log(2.0)

def interp_faces(extended, axis_index, cell_count):

    def shifted(offset):
        return lax.slice_in_dim(extended, offset, offset + cell_count + 1, axis=axis_index)
    return (37.0 * (shifted(2) + shifted(3)) - 8.0 * (shifted(1) + shifted(4)) + (shifted(0) + shifted(5))) / 60.0

def face_sines(first_row, cell_count, total_lat):
    global_row = first_row - 1 + jnp.arange(cell_count + 1, dtype=jnp.int32)
    inside = (global_row >= 0) & (global_row < total_lat - 1)
    return jnp.where(inside, jnp.sin(math.pi * (global_row + 1).astype(jnp.float32) / total_lat), 0.0)

def cell_sines(first_row, cell_count, total_lat):
    global_row = first_row + jnp.arange(cell_count, dtype=jnp.int32)
    return jnp.sin(math.pi * (global_row.astype(jnp.float32) + 0.5) / total_lat)

def tendencies(lat_ent, lat_mer, lon_ent, lon_zon, first_row, total_lat):
    row_count = lat_ent.shape[1] - 6
    col_count = lon_ent.shape[2] - 6
    face_sine = face_sines(first_row, row_count, total_lat)[None, :, None]
    cell_sine = cell_sines(first_row, row_count, total_lat)[None, :, None]
    mer_faces = lat_mer[:, 2:row_count + 3, :] * face_sine
    merid_term = mer_faces * interp_faces(lat_ent, 1, row_count)
    zon_faces = lon_zon[:, :, 2:col_count + 3]
    zonal_term = zon_faces * interp_faces(lon_ent, 2, col_count)
    ent_tend = -(zonal_term[:, :, 1:] - zonal_term[:, :, :-1] + (merid_term[:, 1:] - merid_term[:, :-1]) / cell_sine)
    pres_tend = -sound_factor * (zon_faces[:, :, 1:] - zon_faces[:, :, :-1] + (mer_faces[:, 1:] - mer_faces[:, :-1]) / cell_sine)
    return (ent_tend, pres_tend)

def fourier_tables(order_slot, lon_count):
    longitude = jnp.arange(lon_count, dtype=jnp.int32)
    product = order_slot[None, :] * longitude[:, None] % lon_count
    angles = 2.0 * math.pi / lon_count * product.astype(jnp.float32)
    stacked = jnp.stack((jnp.cos(angles), jnp.sin(angles)), axis=2)
    scales = jnp.where(order_slot == 0, 1.0, 2.0) / lon_count
    forward_table = stacked.reshape(lon_count, -1).astype(jnp.bfloat16)
    inverse_table = (stacked * scales[None, :, None]).reshape(lon_count, -1).T.astype(jnp.bfloat16)
    return (forward_table, inverse_table)

def legendre_tables(orders, total_lat, degree_count):
    colatitude = math.pi * (jnp.arange(total_lat, dtype=jnp.float32) + 0.5) / total_lat
    cosine = jnp.cos(colatitude)[None, :]
    sine_row = jnp.sin(colatitude)
    weights = (sine_row * (math.pi / total_lat))[None, :]
    order_f = orders.astype(jnp.float32)[:, None]
    log_start = -0.5 * math.log(2.0) + 0.5 * (lax.lgamma(order_f + 1.5) - gamma_three_halves - lax.lgamma(order_f + 1.0)) + order_f * jnp.log(sine_row)[None, :]

    def block_step(state_in, block_index):
        prev_vals, curr_vals, log_scale = state_in
        analysis_rows = []
        synthesis_rows = []
        for inner_step in range(16):
            degree = block_index * 16 + inner_step
            deg_f = degree.astype(jnp.float32)
            started = orders[:, None] == degree
            running = orders[:, None] < degree
            denom_a = jnp.maximum(deg_f * deg_f - order_f * order_f, 1.0)
            coef_a = jnp.where(running, jnp.sqrt(jnp.maximum(4.0 * deg_f * deg_f - 1.0, 0.0) / denom_a), 0.0)
            numer_b = jnp.maximum((deg_f - 1.0) * (deg_f - 1.0) - order_f * order_f, 0.0)
            denom_b = jnp.maximum(4.0 * (deg_f - 1.0) * (deg_f - 1.0) - 1.0, 1.0)
            coef_b = coef_a * jnp.sqrt(numer_b / denom_b)
            new_vals = jnp.where(started, 1.0, coef_a * cosine * curr_vals - coef_b * prev_vals)
            log_scale = jnp.where(started, log_start, log_scale)
            values = new_vals * jnp.exp(log_scale)
            analysis_rows.append((values * weights).astype(jnp.bfloat16))
            synthesis_rows.append(values.astype(jnp.bfloat16))
            biggest = jnp.maximum(jnp.abs(curr_vals), jnp.abs(new_vals))
            factor = jnp.where(biggest > 1.0, biggest, 1.0)
            prev_vals = curr_vals / factor
            curr_vals = new_vals / factor
            log_scale = log_scale + jnp.log(factor)
        return ((prev_vals, curr_vals, log_scale), (jnp.stack(analysis_rows, axis=1), jnp.stack(synthesis_rows, axis=1)))
    initial = jnp.zeros((orders.shape[0], total_lat), jnp.float32)
    block_ids = jnp.arange(degree_count // 16, dtype=jnp.int32)
    ignored, tables = lax.scan(block_step, (initial, initial, initial), block_ids)
    return (tables[0], tables[1])

def reference(entropy, zonal_flux, meridional_flux, start_entropy, start_pressure, order_slot):

    def level_terms(fields):
        ent_level, zon_level, mer_level = fields
        lat_ent = jnp.pad(ent_level, ((3, 3), (0, 0)))[None]
        lat_mer = jnp.pad(mer_level, ((3, 3), (0, 0)))[None]
        lon_ent = jnp.pad(ent_level, ((0, 0), (3, 3)), mode='wrap')[None]
        lon_zon = jnp.pad(zon_level, ((0, 0), (3, 3)), mode='wrap')[None]
        ent_tend, pres_tend = tendencies(lat_ent, lat_mer, lon_ent, lon_zon, 0, NLAT)
        return (ent_tend[0], pres_tend[0])
    ent_tend, pres_tend = lax.map(level_terms, (entropy, zonal_flux, meridional_flux))
    tend_items = jnp.concatenate((ent_tend[:FLEV], pres_tend[:FLEV])).astype(jnp.bfloat16)
    forward_table, inverse_table = fourier_tables(order_slot, NLON)
    fourier = jnp.dot(tend_items.reshape(ITEMS * NLAT, NLON), forward_table, preferred_element_type=jnp.float32).astype(jnp.bfloat16)
    fourier = jnp.transpose(fourier.reshape(ITEMS, NLAT, ORDERS, 2), (2, 0, 3, 1))
    group_size = ORDERS // (N_LAT * N_LONR)
    blocks = fourier.reshape(ORDERS // group_size, group_size, ITEMS, 2, NLAT)
    slot_orders = order_slot.reshape(ORDERS // group_size, group_size)
    degree_blocks = ORDERS // 16

    def per_block(pair):
        spec_block, orders = pair
        analysis, synthesis = legendre_tables(orders, NLAT, ORDERS)
        coefficients = jnp.einsum('bolj,oirj->oirbl', analysis.astype(jnp.float32), spec_block.astype(jnp.float32))
        coefficients = coefficients.reshape(group_size, ITEMS, 2, ORDERS)
        rounded = lax.optimization_barrier(coefficients.astype(jnp.bfloat16))
        rounded = rounded.reshape(group_size, ITEMS, 2, degree_blocks, 16)
        returned = jnp.einsum('oirbl,bolj->oirj', rounded.astype(jnp.float32), synthesis.astype(jnp.float32)).astype(jnp.bfloat16)
        return (coefficients, returned)
    coefficients, returned = lax.map(per_block, (blocks, slot_orders))
    spectrum = coefficients.reshape(ORDERS, ITEMS, 2, ORDERS)
    returned = jnp.transpose(returned.reshape(ORDERS, ITEMS, 2, NLAT), (1, 3, 0, 2)).reshape(ITEMS * NLAT, 2 * ORDERS)
    filt_grid = jnp.dot(returned, inverse_table, preferred_element_type=jnp.float32).astype(jnp.bfloat16)
    filt_grid = filt_grid.reshape(ITEMS, NLAT, NLON).astype(jnp.float32)
    ent_total = jnp.concatenate((filt_grid[:FLEV], ent_tend[FLEV:]))
    pres_total = jnp.concatenate((filt_grid[FLEV:], pres_tend[FLEV:]))
    new_entropy = start_entropy + section_weight * ent_total
    new_pressure = start_pressure + section_weight * pres_total
    return (new_entropy, new_pressure, spectrum)
```

```python
import math

import jax
import jax.numpy as jnp
from jax import lax
from jax.experimental import pallas as pl
from jax.experimental.pallas import tpu as pltpu
from jax.sharding import PartitionSpec as P

FLEV = 32
LEV = 40
NLAT = 1024
NLON = 2048
ORDERS = 768
PAIRS = ORDERS // 2
ROWS = 128
COLS = 128
F32 = jnp.float32
BF16 = jnp.bfloat16

gamma_three_halves = 0.5 * math.log(math.pi) - math.log(2.0)


def lane_ids(shape):
    return lax.broadcasted_iota(jnp.int32, shape, len(shape) - 1)


def edges_kernel(s_ref, u_ref, v_ref, east_ref, west_ref, south_ref, north_ref):
    lane = lane_ids((8, 128))

    def one_pair(q, carry):
        east = jnp.zeros((8, 128), F32)
        west = jnp.zeros((8, 128), F32)
        for i in range(32):
            s = s_ref[2 * q + i // 16, pl.ds(8 * (i % 16), 8), :]
            u = u_ref[2 * q + i // 16, pl.ds(8 * (i % 16), 8), :]
            s_end = pltpu.roll(s, (4 * i - 125) % 128, 1)
            u_end = pltpu.roll(u, (4 * i + 3 - 127) % 128, 1)
            s_top = pltpu.roll(s, 4 * i, 1) if i else s
            mine = (lane >= 4 * i) & (lane < 4 * i + 3)
            east = jnp.where(mine, s_end, jnp.where(lane == 4 * i + 3, u_end, east))
            west = jnp.where(mine, s_top, west)
        east_ref[q] = east
        west_ref[q] = west
        return carry

    lax.fori_loop(0, 4, one_pair, 0)
    for lev in range(8):
        south_ref[lev, 0:3, :] = s_ref[lev, 125:128, :]
        south_ref[lev, 3:4, :] = v_ref[lev, 7:8, :]
        north_ref[lev] = s_ref[lev, 0:4, :]


def edges(entropy, zonal, merid):
    whole = pl.BlockSpec((8, ROWS, COLS), lambda g: (g, 0, 0))
    return pl.pallas_call(
        edges_kernel,
        grid=(LEV // 8,),
        in_specs=[whole, whole, pl.BlockSpec((8, 8, COLS), lambda g: (g, ROWS // 8 - 1, 0))],
        out_specs=[
            pl.BlockSpec((4, 8, 128), lambda g: (g, 0, 0)),
            pl.BlockSpec((4, 8, 128), lambda g: (g, 0, 0)),
            pl.BlockSpec((8, 4, 128), lambda g: (g, 0, 0)),
            pl.BlockSpec((8, 4, 128), lambda g: (g, 0, 0)),
        ],
        out_shape=[
            jax.ShapeDtypeStruct((LEV // 2, 8, 128), F32),
            jax.ShapeDtypeStruct((LEV // 2, 8, 128), F32),
            jax.ShapeDtypeStruct((LEV, 4, 128), F32),
            jax.ShapeDtypeStruct((LEV, 4, 128), F32),
        ],
        name="edges",
    )(entropy, zonal, merid)


def stencil(x0, x1, x2, x3, x4, x5):
    return (37.0 * (x2 + x3) - 8.0 * (x1 + x4) + (x0 + x5)) * (1.0 / 60.0)


def tend_kernel(
    s_ref, u_ref, v_ref, hw_ref, he_ref, ow_ref, hn_ref, hs_ref, fs_ref, rc_ref,
    item_ref, ent_ref, pres_ref, ext, mext,
):
    step = pl.program_id(0)
    lane = lane_ids((ROWS, COLS))
    last = lane == COLS - 1

    def level(q, half):
        lev = 2 * q + half
        s = s_ref[lev]
        u = u_ref[lev]
        west = hw_ref[q]
        east = he_ref[q]
        own = ow_ref[q]
        edge = stencil(
            pltpu.roll(west, 3, 1), pltpu.roll(west, 2, 1), pltpu.roll(west, 1, 1),
            pltpu.roll(own, 3, 1), pltpu.roll(own, 2, 1), pltpu.roll(own, 1, 1),
        )
        edge = edge * west
        tiles = range(16 * half, 16 * half + 16)
        s_west = jnp.concatenate([pltpu.roll(west, (125 - 4 * i) % 128, 1) for i in tiles])
        u_west = jnp.concatenate([pltpu.roll(west, (124 - 4 * i) % 128, 1) for i in tiles])
        z_west = jnp.concatenate([pltpu.roll(edge, (124 - 4 * i) % 128, 1) for i in tiles])
        s_east = jnp.concatenate([pltpu.roll(east, (128 - 4 * i) % 128, 1) for i in tiles])
        e_face = stencil(
            pltpu.roll(jnp.where(lane >= COLS - 2, s_west, s), 2, 1),
            pltpu.roll(jnp.where(last, s_west, s), 1, 1),
            s,
            pltpu.roll(jnp.where(lane < 1, s_east, s), 127, 1),
            pltpu.roll(jnp.where(lane < 2, s_east, s), 126, 1),
            pltpu.roll(jnp.where(lane < 3, s_east, s), 125, 1),
        )
        z = u * e_face
        dz = z - pltpu.roll(jnp.where(last, z_west, z), 1, 1)
        du = u - pltpu.roll(jnp.where(last, u_west, u), 1, 1)
        ext[5:8, :] = hn_ref[lev, 0:3, :]
        ext[8:136, :] = s
        ext[136:139, :] = hs_ref[lev, 0:3, :]
        n_face = stencil(*[ext[6 + o:134 + o, :] for o in range(6)])
        n_top = stencil(*[ext[5 + o:6 + o, :] for o in range(6)])
        fv = v_ref[lev] * fs_ref[8:136, :]
        fv_top = hn_ref[lev, 3:4, :] * fs_ref[7:8, :]
        m = fv * n_face
        mext[0, 7:8, :] = fv_top * n_top
        mext[0, 8:136, :] = m
        mext[1, 7:8, :] = fv_top
        mext[1, 8:136, :] = fv
        rc = rc_ref[...]
        ent = -(dz + (m - mext[0, 7:135, :]) * rc)
        pres = -0.3 * (du + (fv - mext[1, 7:135, :]) * rc)
        return lev, ent, pres

    @pl.when(step < FLEV // 8)
    def _():
        def body(q, carry):
            for half in range(2):
                lev, ent, pres = level(q, half)
                item_ref[0, lev] = ent.astype(BF16)
                item_ref[1, lev] = pres.astype(BF16)
            return carry

        lax.fori_loop(0, 4, body, 0)

    @pl.when(step == FLEV // 8)
    def _():
        def body(q, carry):
            for half in range(2):
                lev, ent, pres = level(q, half)
                ent_ref[lev] = ent
                pres_ref[lev] = pres
            return carry

        lax.fori_loop(0, 4, body, 0)


def tendencies(s, u, v, from_west, from_east, own_west, from_north, from_south, fs, rc):
    whole = pl.BlockSpec((8, ROWS, COLS), lambda g: (g, 0, 0))
    packed = pl.BlockSpec((4, 8, 128), lambda g: (g, 0, 0))
    rows4 = pl.BlockSpec((8, 4, 128), lambda g: (g, 0, 0))
    tail = pl.BlockSpec((8, ROWS, COLS), lambda g: (0, 0, 0))
    return pl.pallas_call(
        tend_kernel,
        grid=(LEV // 8,),
        in_specs=[
            whole, whole, whole, packed, packed, packed, rows4, rows4,
            pl.BlockSpec((136, 128), lambda g: (0, 0)),
            pl.BlockSpec((128, 128), lambda g: (0, 0)),
        ],
        out_specs=[
            pl.BlockSpec((2, 8, ROWS, COLS), lambda g: (0, jnp.minimum(g, FLEV // 8 - 1), 0, 0)),
            tail, tail,
        ],
        out_shape=[
            jax.ShapeDtypeStruct((2, FLEV, ROWS, COLS), BF16),
            jax.ShapeDtypeStruct((LEV - FLEV, ROWS, COLS), F32),
            jax.ShapeDtypeStruct((LEV - FLEV, ROWS, COLS), F32),
        ],
        scratch_shapes=[pltpu.VMEM((144, 128), F32), pltpu.VMEM((2, 136, 128), F32)],
        name="tendencies",
    )(s, u, v, from_west, from_east, own_west, from_north, from_south, fs, rc)


def table_kernel(base_ref, turn_ref, out_ref):
    for par in range(2):
        c = base_ref[par, 0]
        s = base_ref[par, 1]
        for b in range(8):
            tc = jnp.broadcast_to(turn_ref[par, :, b:b + 1], c.shape)
            ts = jnp.broadcast_to(turn_ref[par, :, 8 + b:9 + b], c.shape)
            out_ref[par, 0, :, 128 * b:128 * b + 128] = (c * tc - s * ts).astype(BF16)
            out_ref[par, 1, :, 128 * b:128 * b + 128] = (s * tc + c * ts).astype(BF16)


def fourier_table(even_odd):
    def angles(steps):
        product = (even_odd[:, :, None] * steps[None, None, :]) % NLON
        return (2.0 * math.pi / NLON) * product.astype(F32)

    near = angles(jnp.arange(128, dtype=jnp.int32))
    far = angles(128 * jnp.arange(8, dtype=jnp.int32))
    base = jnp.stack((jnp.cos(near), jnp.sin(near)), axis=1)
    turn = jnp.concatenate((jnp.cos(far), jnp.sin(far)), axis=2)
    tile = 96
    return pl.pallas_call(
        table_kernel,
        grid=(PAIRS // tile,),
        in_specs=[
            pl.BlockSpec((2, 2, tile, 128), lambda g: (0, 0, g, 0)),
            pl.BlockSpec((2, tile, 16), lambda g: (0, g, 0)),
        ],
        out_specs=pl.BlockSpec((2, 2, tile, NLON // 2), lambda g: (0, 0, g, 0)),
        out_shape=jax.ShapeDtypeStruct((2, 2, PAIRS, NLON // 2), BF16),
        name="longitude_table",
    )(base, turn)


def forward_kernel(x_ref, t_ref, o_ref, fold, rows):
    @pl.when(pl.program_id(0) == 0)
    def _():
        for a in range(4):
            for b in range(8):
                lo = x_ref[b, a].astype(F32)
                hi = x_ref[b + 8, a].astype(F32)
                fold[0, 128 * a:128 * a + 128, 128 * b:128 * b + 128] = (lo + hi).astype(BF16)
                fold[1, 128 * a:128 * a + 128, 128 * b:128 * b + 128] = (lo - hi).astype(BF16)

    tile = t_ref.shape[2]
    for par in range(2):
        for ri in range(2):
            res = lax.dot_general(
                t_ref[par, ri], fold[par], (((1,), (1,)), ((), ())), preferred_element_type=F32
            )
            for a in range(4):
                rows[pl.ds(8 * par + 2 * a + ri, tile, stride=16), :] = res[:, 128 * a:128 * a + 128]
    o_ref[...] = rows[...].reshape(o_ref.shape).astype(BF16)


def forward(x, table):
    tile = 96
    return pl.pallas_call(
        forward_kernel,
        grid=(PAIRS // tile,),
        in_specs=[
            pl.BlockSpec((16, 4, 128, 128), lambda g: (0, 0, 0, 0)),
            pl.BlockSpec((2, 2, tile, NLON // 2), lambda g: (0, 0, g, 0)),
        ],
        out_specs=pl.BlockSpec((tile // 3, 48, 128), lambda g: (g, 0, 0)),
        out_shape=jax.ShapeDtypeStruct((128, 48, 128), BF16),
        scratch_shapes=[
            pltpu.VMEM((2, 512, NLON // 2), BF16),
            pltpu.VMEM((16 * tile, 128), F32),
        ],
        name="forward",
    )(x, table)


CHUNK = 128


def legendre_kernel(a_ref, b_ref, m_ref, cos_ref, start_ref, w_ref, ana_ref, syn_ref, rows, state):
    chunk = pl.program_id(0)
    upper = lax.broadcasted_iota(jnp.int32, (8, 128), 0) < 4

    @pl.when(chunk == 0)
    def _():
        state[...] = jnp.zeros_like(state)

    cosine = [cos_ref[8 * v:8 * v + 8, :] for v in range(3)]
    orders = [m_ref[8 * v:8 * v + 8, :] for v in range(3)]

    def body(it, carry):
        prev, curr, logs, scale = carry
        for k in range(4):
            local = it * 4 + k
            degree = chunk * CHUNK + local
            nxt = []
            new_logs = []
            new_scale = []
            for v in range(3):
                at = degree * 6 + 2 * v
                a = jnp.where(upper, a_ref[at], a_ref[at + 1])
                b = jnp.where(upper, b_ref[at], b_ref[at + 1])
                first = orders[v] == degree
                start = start_ref[8 * v:8 * v + 8, :]
                val = jnp.where(first, 1.0, (a * cosine[v]) * curr[v] - b * prev[v])
                lg = jnp.where(first, start, logs[v])
                sc = jnp.where(first, start_ref[24 + 8 * v:32 + 8 * v, :], scale[v])
                row = pl.multiple_of(local * 24, 8) + 8 * v
                rows[pl.ds(row, 8), :] = val * sc
                nxt.append(val)
                new_logs.append(lg)
                new_scale.append(sc)
            prev, curr, logs, scale = curr, nxt, new_logs, new_scale
        grow = [jnp.maximum(1.0, jnp.maximum(jnp.abs(p), jnp.abs(c))) for p, c in zip(prev, curr)]
        inv = [1.0 / g for g in grow]
        prev = [p * i for p, i in zip(prev, inv)]
        curr = [c * i for c, i in zip(curr, inv)]
        logs = [l + jnp.log(g) for l, g in zip(logs, grow)]
        scale = [jnp.where(s > -1.0, jnp.where(o <= chunk * CHUNK + it * 4 + 3, jnp.exp(l), 0.0), 0.0)
                 for s, l, o in zip(scale, logs, orders)]
        return prev, curr, logs, scale

    init = tuple([state[24 * n + 8 * v:24 * n + 8 * v + 8, :] for v in range(3)] for n in range(4))
    final = lax.fori_loop(0, CHUNK // 4, body, init)
    for n in range(4):
        for v in range(3):
            state[24 * n + 8 * v:24 * n + 8 * v + 8, :] = final[n][v]
    for o in range(6):
        for jb in range(4):
            val = rows[pl.ds(4 * o + jb, CHUNK, stride=24), :]
            syn_ref[o, :, 128 * jb:128 * jb + 128] = val.astype(BF16)
            ana_ref[o, :, 128 * jb:128 * jb + 128] = (val * w_ref[jb:jb + 1, :]).astype(BF16)


def legendre_tables(orders):
    half = NLAT // 2
    colatitude = math.pi * (jnp.arange(half, dtype=F32) + 0.5) / NLAT
    sine = jnp.sin(colatitude)
    order_f = orders.astype(F32)
    log_start = (
        -0.5 * math.log(2.0)
        + 0.5 * (lax.lgamma(order_f + 1.5) - gamma_three_halves - lax.lgamma(order_f + 1.0))
    )[:, None] + order_f[:, None] * jnp.log(sine)[None, :]
    log_start = log_start.reshape(24, 128)
    start = jnp.concatenate((log_start, jnp.exp(log_start)))
    cosine = jnp.tile(jnp.cos(colatitude).reshape(4, 128), (6, 1))
    weight = (sine * (math.pi / NLAT)).reshape(4, 128)
    deg = jnp.arange(ORDERS, dtype=F32)[:, None]
    running = orders[None, :] < jnp.arange(ORDERS, dtype=jnp.int32)[:, None]
    denom_a = jnp.maximum(deg * deg - order_f * order_f, 1.0)
    coef_a = jnp.where(running, jnp.sqrt(jnp.maximum(4.0 * deg * deg - 1.0, 0.0) / denom_a), 0.0)
    numer_b = jnp.maximum((deg - 1.0) * (deg - 1.0) - order_f * order_f, 0.0)
    denom_b = jnp.maximum(4.0 * (deg - 1.0) * (deg - 1.0) - 1.0, 1.0)
    coef_b = coef_a * jnp.sqrt(numer_b / denom_b)
    order_rows = jnp.broadcast_to(jnp.repeat(orders, 4)[:, None], (24, 128))
    smem = pl.BlockSpec(memory_space=pltpu.SMEM)
    full = pl.BlockSpec((24, 128), lambda g: (0, 0))
    table = pl.BlockSpec((6, CHUNK, half), lambda g: (0, g, 0))
    return pl.pallas_call(
        legendre_kernel,
        grid=(ORDERS // CHUNK,),
        in_specs=[
            smem, smem, full, full,
            pl.BlockSpec((48, 128), lambda g: (0, 0)),
            pl.BlockSpec((4, 128), lambda g: (0, 0)),
        ],
        out_specs=[table, table],
        out_shape=[jax.ShapeDtypeStruct((6, ORDERS, half), BF16)] * 2,
        scratch_shapes=[pltpu.VMEM((CHUNK * 24, 128), F32), pltpu.VMEM((96, 128), F32)],
        name="legendre_tables",
    )(coef_a.reshape(-1), coef_b.reshape(-1), order_rows, cosine, start, weight)


def filter_kernel(slot_ref, ord_ref, f_ref, ana_ref, syn_ref, spec_ref, back_ref):
    o = pl.program_id(0)
    order = ord_ref[o]
    sub = lax.broadcasted_iota(jnp.int32, (128, 128), 0)
    flip = jnp.where(sub + lane_ids((128, 128)) == 127, 1.0, 0.0).astype(BF16)
    plus = []
    minus = []
    for c in range(4):
        north = f_ref[c, :, 0].astype(F32).reshape(128, 128)
        south = f_ref[7 - c, :, 0].astype(F32).reshape(128, 128).astype(BF16)
        south = jnp.dot(south, flip, preferred_element_type=F32)
        plus.append((north + south).astype(BF16))
        minus.append((north - south).astype(BF16))
    both = jnp.concatenate(
        [jnp.concatenate(plus, axis=1), jnp.concatenate(minus, axis=1)], axis=0
    )
    coef = lax.dot_general(
        both, ana_ref[0], (((1,), (1,)), ((), ())), preferred_element_type=F32
    )
    even = ((lane_ids((128, ORDERS)) - order) & 1) == 0
    spec = jnp.where(even, coef[:128], coef[128:])
    spec_ref[0] = spec
    parts = jnp.concatenate([jnp.where(even, spec, 0.0), jnp.where(even, 0.0, spec)], axis=0)
    grid = jnp.dot(parts.astype(BF16), syn_ref[0], preferred_element_type=F32)
    factor = jnp.where(order == 0, 0.5, 1.0)
    north = (grid[:128] + grid[128:]) * factor
    south = ((grid[:128] - grid[128:]) * factor).astype(BF16)
    for c in range(4):
        cut = slice(128 * c, 128 * c + 128)
        back_ref[c, :, 0] = north[:, cut].reshape(16, 8, 128).astype(BF16)
        turned = jnp.dot(south[:, cut], flip, preferred_element_type=F32)
        back_ref[7 - c, :, 0] = turned.reshape(16, 8, 128).astype(BF16)


def legendre_filter(fourier, analysis, synthesis, orders, slots):
    half = NLAT // 2
    blocks = pl.BlockSpec((8, 16, 1, 8, 128), lambda o, *_: (0, 0, o, 0, 0))
    table = pl.BlockSpec((1, ORDERS, half), lambda o, *_: (o, 0, 0))
    return pl.pallas_call(
        filter_kernel,
        grid_spec=pltpu.PrefetchScalarGridSpec(
            num_scalar_prefetch=2,
            grid=(6,),
            in_specs=[blocks, table, table],
            out_specs=[
                pl.BlockSpec((1, 128, ORDERS), lambda o, slot, order: (slot[o], 0, 0)),
                blocks,
            ],
        ),
        out_shape=[
            jax.ShapeDtypeStruct((6, 128, ORDERS), F32),
            jax.ShapeDtypeStruct((8, 16, 6, 8, 128), BF16),
        ],
        name="legendre_filter",
    )(slots, orders, fourier, analysis, synthesis)


def inverse_kernel(y_ref, t_ref, o_ref, rows):
    @pl.when(pl.program_id(0) == 0)
    def _():
        rows[...] = y_ref[...].astype(F32).reshape(rows.shape)

    a = pl.program_id(0)
    sums = []
    for par in range(2):
        parts = [rows[pl.ds(8 * par + 2 * a + ri, PAIRS, stride=16), :].astype(BF16) for ri in range(2)]
        total = None
        for ri in range(2):
            res = lax.dot_general(
                parts[ri], t_ref[par, ri], (((0,), (0,)), ((), ())), preferred_element_type=F32
            )
            total = res if total is None else total + res
        sums.append(total * (2.0 / NLON))
    low = (sums[0] + sums[1]).astype(BF16)
    high = (sums[0] - sums[1]).astype(BF16)
    for b in range(8):
        o_ref[b, 0] = low[:, 128 * b:128 * b + 128]
        o_ref[b + 8, 0] = high[:, 128 * b:128 * b + 128]


def inverse(y, table):
    return pl.pallas_call(
        inverse_kernel,
        grid=(4,),
        in_specs=[
            pl.BlockSpec((128, 48, 128), lambda a: (0, 0, 0)),
            pl.BlockSpec((2, 2, PAIRS, NLON // 2), lambda a: (0, 0, 0, 0)),
        ],
        out_specs=pl.BlockSpec((16, 1, 128, 128), lambda a: (0, a, 0, 0)),
        out_shape=jax.ShapeDtypeStruct((16, 4, 128, 128), BF16),
        scratch_shapes=[pltpu.VMEM((128 * 48, 128), F32)],
        name="inverse",
    )(y, table)


def update_kernel(se_ref, sp_ref, f_ref, et_ref, pt_ref, oe_ref, op_ref):
    @pl.when(pl.program_id(0) < FLEV // 8)
    def _():
        oe_ref[...] = se_ref[...] + 0.5 * f_ref[0].astype(F32)
        op_ref[...] = sp_ref[...] + 0.5 * f_ref[1].astype(F32)

    @pl.when(pl.program_id(0) == FLEV // 8)
    def _():
        oe_ref[...] = se_ref[...] + 0.5 * et_ref[...]
        op_ref[...] = sp_ref[...] + 0.5 * pt_ref[...]


def update(start_entropy, start_pressure, filtered, ent_tail, pres_tail):
    whole = pl.BlockSpec((8, ROWS, COLS), lambda g: (g, 0, 0))
    tail = pl.BlockSpec((8, ROWS, COLS), lambda g: (0, 0, 0))
    return pl.pallas_call(
        update_kernel,
        grid=(LEV // 8,),
        in_specs=[
            whole, whole,
            pl.BlockSpec((2, 8, ROWS, COLS), lambda g: (0, jnp.minimum(g, FLEV // 8 - 1), 0, 0)),
            tail, tail,
        ],
        out_specs=[whole, whole],
        out_shape=[jax.ShapeDtypeStruct((LEV, ROWS, COLS), F32)] * 2,
        name="update",
    )(start_entropy, start_pressure, filtered, ent_tail, pres_tail)


def lat_factors():
    first = lax.axis_index("lat") * ROWS
    face = first - 8 + jnp.arange(136, dtype=jnp.int32)
    inside = (face >= 0) & (face < NLAT - 1)
    fs = jnp.where(inside, jnp.sin(math.pi * (face + 1).astype(F32) / NLAT), 0.0)
    row = first + jnp.arange(ROWS, dtype=jnp.int32)
    rc = 1.0 / jnp.sin(math.pi * (row.astype(F32) + 0.5) / NLAT)
    return jnp.broadcast_to(fs[:, None], (136, 128)), jnp.broadcast_to(rc[:, None], (128, 128))


def per_device(entropy, zonal_flux, meridional_flux, start_entropy, start_pressure, order_slot):
    n_lat = lax.axis_size("lat")
    n_lon = lax.axis_size("lonr")
    pairs = order_slot.reshape(PAIRS, 2)
    first_even = (pairs[:, 0] % 2) == 0
    even = jnp.where(first_even, pairs[:, 0], pairs[:, 1])
    odd = jnp.where(first_even, pairs[:, 1], pairs[:, 0])
    block = lax.axis_index("lat") * n_lon + lax.axis_index("lonr")
    both = jnp.stack((even, odd), axis=1)
    orders = lax.dynamic_slice_in_dim(both, block * 3, 3).reshape(6)
    swap = jnp.where(first_even, 0, 1).astype(jnp.int32)
    swap = lax.dynamic_slice_in_dim(swap, block * 3, 3)
    base = 2 * jnp.arange(3, dtype=jnp.int32)
    slots = jnp.stack((base + swap, base + 1 - swap), axis=1).reshape(6)

    east, west, south, north = edges(entropy, zonal_flux, meridional_flux)
    ring = range(n_lon)
    from_west = lax.ppermute(east, "lonr", [(i, (i + 1) % n_lon) for i in ring])
    from_east = lax.ppermute(west, "lonr", [((i + 1) % n_lon, i) for i in ring])
    from_north = lax.ppermute(south, "lat", [(i, i + 1) for i in range(n_lat - 1)])
    from_south = lax.ppermute(north, "lat", [(i + 1, i) for i in range(n_lat - 1)])
    table = fourier_table(jnp.stack((even, odd)))
    fs, rc = lat_factors()
    items, ent_tail, pres_tail = tendencies(
        entropy, zonal_flux, meridional_flux, from_west, from_east, west, from_north, from_south, fs, rc
    )
    grid = lax.all_to_all(
        items.reshape(16, 4, ROWS, COLS), "lonr", split_axis=0, concat_axis=0, tiled=True
    )
    analysis, synthesis = legendre_tables(orders)
    spectral = forward(grid, table)
    spectral = lax.all_to_all(
        spectral, ("lat", "lonr"), split_axis=0, concat_axis=0, tiled=True
    )
    spectrum, back = legendre_filter(
        spectral.reshape(8, 16, 6, 8, 128), analysis, synthesis, orders, slots
    )
    back = lax.all_to_all(
        back.reshape(128, 48, 128), ("lat", "lonr"), split_axis=0, concat_axis=0, tiled=True
    )
    filtered = inverse(back, table)
    filtered = lax.all_to_all(filtered, "lonr", split_axis=0, concat_axis=0, tiled=True)
    new_entropy, new_pressure = update(
        start_entropy, start_pressure, filtered.reshape(2, FLEV, ROWS, COLS), ent_tail, pres_tail
    )
    return new_entropy, new_pressure, spectrum.reshape(6, 64, 2, ORDERS)


def solution(mesh):
    cube = P(None, "lat", "lonr")
    return jax.shard_map(
        per_device,
        mesh=mesh,
        in_specs=(cube, cube, cube, cube, cube, P()),
        out_specs=(cube, cube, P(("lat", "lonr"), None, None, None)),
        check_vma=False,
    )
```

```python
import math

import jax
import jax.numpy as jnp
from jax import lax
from jax.experimental import pallas as pl
from jax.experimental.pallas import tpu as pltpu
import numpy as np
from jax.sharding import PartitionSpec as P

FLEV = 32
LEV = 40
NLAT = 1024
NLON = 2048
ORDERS = 768
PAIRS = ORDERS // 2
ROWS = 128
COLS = 128
F32 = jnp.float32
BF16 = jnp.bfloat16

gamma_three_halves = 0.5 * math.log(math.pi) - math.log(2.0)


def vmem(mib):
    return pltpu.CompilerParams(vmem_limit_bytes=mib << 20)


IN_VMEM = pl.BlockSpec(memory_space=pltpu.VMEM)


def in_vmem(x):
    return pltpu.with_memory_space_constraint(x, pltpu.VMEM)


def lane_ids(shape):
    return lax.broadcasted_iota(jnp.int32, shape, len(shape) - 1)


def edges_kernel(
    first_ref, s_any, u_any, v_ref, east_ref, west_ref, south_ref, north_ref, fs_ref, rc_ref,
    s_ref, u_ref, sems
):
    lane = lane_ids((8, 128))
    group = lane >> 3
    flux = (lane & 7) == 7
    parts = LEV // 8

    def fetch(n, g):
        at = pl.ds(8 * g, 8)
        src = (s_any, u_any)[n]
        dst = (s_ref, u_ref)[n]
        return pltpu.make_async_copy(src.at[at], dst.at[at], sems.at[n, g])

    for g in range(parts):
        for n in range(2):
            fetch(n, g).start()
    at = first_ref[0] - 8 + lax.broadcasted_iota(jnp.int32, (136, 128), 0)
    sines = jnp.sin((math.pi / NLAT) * (at + 1).astype(F32))
    fs_ref[...] = jnp.where((at >= 0) & (at < NLAT - 1), sines, 0.0)
    rc_ref[...] = 1.0 / jnp.sin((math.pi / NLAT) * (at[8:].astype(F32) + 0.5))

    def one_pair(q, carry):
        for half in range(2):
            lev = 2 * q + half
            east = jnp.zeros((8, 128), F32)
            west = jnp.zeros((8, 128), F32)
            for i in range(16):
                s = s_ref[lev, pl.ds(8 * i, 8), :]
                u = u_ref[lev, pl.ds(8 * i, 8), :]
                s_end = pltpu.roll(s, (8 * i + 7) % 128, 1)
                u_end = pltpu.roll(u, (8 * i + 8) % 128, 1)
                s_top = pltpu.roll(s, 8 * i, 1) if i else s
                mine = group == i
                east = jnp.where(mine, jnp.where(flux, u_end, s_end), east)
                west = jnp.where(mine, s_top, west)
            east_ref[lev] = east
            west_ref[lev] = west
            south_ref[lev, 0:3, :] = s_ref[lev, 125:128, :]
            north_ref[lev] = s_ref[lev, 0:4, :]
        return carry

    for g in range(parts):
        for n in range(2):
            fetch(n, g).wait()
        lax.fori_loop(4 * g, 4 * g + 4, one_pair, 0)
    for lev in range(LEV):
        south_ref[lev, 3:4, :] = v_ref[lev, 7:8, :]


def edges(first, entropy, zonal, merid):
    anywhere = pl.BlockSpec(memory_space=pl.ANY)
    return pl.pallas_call(
        edges_kernel,
        grid=(1,),
        in_specs=[pl.BlockSpec(memory_space=pltpu.SMEM), anywhere, anywhere, pl.BlockSpec((LEV, 8, COLS), lambda g: (0, ROWS // 8 - 1, 0))],
        out_specs=[pl.BlockSpec((LEV, n, 128), lambda g: (0, 0, 0)) for n in (8, 8, 4, 4)]
        + [pl.BlockSpec((n, 128), lambda g: (0, 0)) for n in (136, 128)],
        out_shape=[
            pltpu.HBM((LEV, 8, 128), F32),
            pltpu.HBM((LEV, 8, 128), F32),
            pltpu.HBM((LEV, 4, 128), F32),
            pltpu.HBM((LEV, 4, 128), F32),
            pltpu.HBM((136, 128), F32),
            pltpu.HBM((128, 128), F32),
        ],
        scratch_shapes=[pltpu.VMEM((LEV, ROWS, COLS), F32)] * 2
        + [pltpu.SemaphoreType.DMA((2, LEV // 8))],
        name="edges",
    )(first, entropy, zonal, merid)


def stencil(x0, x1, x2, x3, x4, x5):
    return (37.0 * (x2 + x3) - 8.0 * (x1 + x4) + (x0 + x5)) * (1.0 / 60.0)


def stencil_matrices():
    weights = {-2: 1.0, -1: -8.0, 0: 37.0, 1: 37.0, 2: -8.0, 3: 1.0}
    along = np.zeros((256, 256), np.float32)
    across = np.zeros((128, 136), np.float32)
    for face in range(128):
        for shift, weight in weights.items():
            cell = face + shift
            along[cell if 0 <= cell < 128 else 128 + cell % 128 if cell >= 128 else 128 + 7 + cell, face] = weight
            across[face, cell if 0 <= cell < 128 else 128 + 4 + cell % 128 if cell >= 128 else 128 + 3 + cell] = weight
    along[128 + 3, 128 + 127] = 1.0
    along[128 + 7, 128] = 1.0
    return along, across


def split(x):
    high = x.astype(BF16)
    return high, (x - high.astype(F32)).astype(BF16)


def tend_kernel(
    s_ref, u_ref, v_ref, hw_ref, he_ref, ow_ref, hn_ref, hs_ref, fs_ref, rc_ref, along_ref, across_ref,
    se_ref, sp_ref, item_ref, ent_ref, pres_ref, cells, face, mext,
):
    step = pl.program_id(0)
    lane = lane_ids((ROWS, COLS))
    small = lane_ids((8, 128)) & 7
    across = across_ref[...]

    def prepare(q, carry):
        for half in range(4):
            lev = 4 * q + half
            west = hw_ref[lev]
            own = ow_ref[lev]
            edge = stencil(
                pltpu.roll(west, 127, 1), pltpu.roll(west, 126, 1), pltpu.roll(west, 125, 1),
                pltpu.roll(own, 3, 1), pltpu.roll(own, 2, 1), pltpu.roll(own, 1, 1),
            )
            edge = edge * pltpu.roll(west, 124, 1)
            rim = jnp.where(small < 3, he_ref[lev], jnp.where(small == 3, edge, west))
            rim = jnp.concatenate([pltpu.roll(rim, (128 - 8 * i) % 128, 1) for i in range(16)])
            s = s_ref[lev]
            s_hi, s_lo = split(s)
            r_hi, r_lo = split(rim)
            at = pl.ds(pl.multiple_of(lev * 128, 128), 128)
            cells[at, 0:128] = s_hi
            cells[at, 128:256] = r_hi
            cells[at, 256:384] = s_lo
            cells[at, 384:512] = r_lo
            h_hi, h_lo = split(jnp.concatenate([hn_ref[lev], hs_ref[lev]]))
            n_face = jnp.dot(
                across, jnp.concatenate([s_hi, s_lo, h_hi, h_lo]), preferred_element_type=F32
            )
            face[lev, :, 256:384] = n_face
        return carry

    lax.fori_loop(0, 2, prepare, 0)
    for part in range(2):
        rows = slice(512 * part, 512 * part + 512)
        res = jnp.dot(cells[rows, :], along_ref[...], preferred_element_type=F32)
        face[4 * part:4 * part + 4, :, 0:256] = res.reshape(4, 128, 256)

    def level(lev, half):
        u = u_ref[lev]
        z = (u * (1.0 / 60.0)) * face[lev, :, 0:128]
        rim = face[lev, :, 128:256]
        dz = z - pltpu.roll(jnp.where(lane == COLS - 1, rim, z), 1, 1)
        du = u - jnp.where(lane == 0, rim, pltpu.roll(u, 1, 1))
        fv = v_ref[lev] * fs_ref[8:136, :]
        fv_top = hn_ref[lev, 3:4, :] * fs_ref[7:8, :]
        top = [hn_ref[lev, o:o + 1, :] for o in range(3)] + [s_ref[lev, o:o + 1, :] for o in range(3)]
        m = fv * (face[lev, :, 256:384] * (1.0 / 60.0))
        mext[half, 0, 7:8, :] = fv_top * stencil(*top)
        mext[half, 0, 8:136, :] = m
        mext[half, 1, 7:8, :] = fv_top
        mext[half, 1, 8:136, :] = fv
        rc = rc_ref[...]
        ent = -(dz + (m - mext[half, 0, 7:135, :]) * rc)
        pres = -0.3 * (du + (fv - mext[half, 1, 7:135, :]) * rc)
        return ent, pres

    @pl.when(step < FLEV // 8)
    def _():
        def body(q, carry):
            for half in range(4):
                ent, pres = level(4 * q + half, half)
                item_ref[0, 4 * q + half] = ent.astype(BF16)
                item_ref[1, 4 * q + half] = pres.astype(BF16)
            return carry

        lax.fori_loop(0, 2, body, 0)

    @pl.when(step == FLEV // 8)
    def _():
        def body(q, carry):
            for half in range(4):
                ent, pres = level(4 * q + half, half)
                lev = 4 * q + half
                ent_ref[lev] = se_ref[lev] + 0.5 * ent
                pres_ref[lev] = sp_ref[lev] + 0.5 * pres
            return carry

        lax.fori_loop(0, 2, body, 0)


def tendencies(
    s, u, v, from_west, from_east, own_west, from_north, from_south, fs, rc, start_entropy, start_pressure
):
    whole = pl.BlockSpec((8, ROWS, COLS), lambda g: (g, 0, 0))
    packed = pl.BlockSpec((8, 8, 128), lambda g: (g, 0, 0))
    rows4 = pl.BlockSpec((8, 4, 128), lambda g: (g, 0, 0))
    tail = pl.BlockSpec((8, ROWS, COLS), lambda g: (FLEV // 8, 0, 0))
    along, across = stencil_matrices()
    along = jnp.asarray(np.concatenate((along, along)), BF16)
    across = np.concatenate(
        (across[:, :128], across[:, :128], across[:, 128:], across[:, 128:]), axis=1
    )
    return pl.pallas_call(
        tend_kernel,
        grid=(LEV // 8,),
        in_specs=[
            whole, whole, whole, packed, packed, packed, rows4, rows4,
            pl.BlockSpec((136, 128), lambda g: (0, 0)),
            pl.BlockSpec((128, 128), lambda g: (0, 0)),
            pl.BlockSpec((512, 256), lambda g: (0, 0)),
            pl.BlockSpec((128, 272), lambda g: (0, 0)),
            tail, tail,
        ],
        out_specs=[
            pl.BlockSpec((2, 8, ROWS, COLS), lambda g: (0, jnp.minimum(g, FLEV // 8 - 1), 0, 0)),
            tail, tail,
        ],
        out_shape=[
            pltpu.HBM((2, FLEV, ROWS, COLS), BF16),
            pltpu.HBM((LEV, ROWS, COLS), F32),
            pltpu.HBM((LEV, ROWS, COLS), F32),
        ],
        scratch_shapes=[
            pltpu.VMEM((1024, 512), BF16),
            pltpu.VMEM((8, 128, 384), F32),
            pltpu.VMEM((4, 2, 136, 128), F32),
        ],
        name="tendencies",
    )(s, u, v, from_west, from_east, own_west, from_north, from_south, fs, rc,
      along, jnp.asarray(across, BF16), start_entropy, start_pressure)


def table_kernel(base_ref, turn_ref, out_ref):
    for par in range(2):
        c = base_ref[par, 0]
        s = base_ref[par, 1]
        for b in range(8):
            tc = jnp.broadcast_to(turn_ref[par, :, b:b + 1], c.shape)
            ts = jnp.broadcast_to(turn_ref[par, :, 8 + b:9 + b], c.shape)
            out_ref[par, 0, :, 128 * b:128 * b + 128] = (c * tc - s * ts).astype(BF16)
            out_ref[par, 1, :, 128 * b:128 * b + 128] = (s * tc + c * ts).astype(BF16)


def fourier_table(even_odd):
    def angles(steps):
        product = (even_odd[:, :, None] * steps[None, None, :]) % NLON
        return (2.0 * math.pi / NLON) * product.astype(F32)

    near = angles(jnp.arange(128, dtype=jnp.int32))
    far = angles(128 * jnp.arange(8, dtype=jnp.int32))
    base = jnp.stack((jnp.cos(near), jnp.sin(near)), axis=1)
    turn = jnp.concatenate((jnp.cos(far), jnp.sin(far)), axis=2)
    tile = 96
    return pl.pallas_call(
        table_kernel,
        grid=(PAIRS // tile,),
        in_specs=[
            pl.BlockSpec((2, 2, tile, 128), lambda g: (0, 0, g, 0)),
            pl.BlockSpec((2, tile, 16), lambda g: (0, g, 0)),
        ],
        out_specs=pl.BlockSpec((2, 2, tile, NLON // 2), lambda g: (0, 0, g, 0)),
        out_shape=pltpu.HBM((2, 2, PAIRS, NLON // 2), BF16),
        name="longitude_table",
    )(base, turn)


def forward_kernel(x_ref, t_ref, o_ref, fold, rows):
    par = pl.program_id(0)
    for a in range(4):
        for b in range(8):
            lo = x_ref[b, a]
            hi = x_ref[b + 8, a]
            fold[128 * a:128 * a + 128, 128 * b:128 * b + 128] = lo + jnp.where(par == 0, hi, -hi)
    res = lax.dot_general(
        t_ref[0].reshape(2 * PAIRS, NLON // 2), fold[...], (((1,), (1,)), ((), ())),
        preferred_element_type=F32,
    )
    for ri in range(2):
        for a in range(4):
            rows[pl.ds(8 * par + 2 * a + ri, PAIRS, stride=16), :] = (
                res[PAIRS * ri:PAIRS * ri + PAIRS, 128 * a:128 * a + 128]
            )

    @pl.when(par == 1)
    def _():
        o_ref[...] = rows[...].reshape(o_ref.shape).astype(BF16)


def forward(x, table):
    return pl.pallas_call(
        forward_kernel,
        grid=(2,),
        in_specs=[
            IN_VMEM,
            pl.BlockSpec((1, 2, PAIRS, NLON // 2), lambda g: (g, 0, 0, 0)),
        ],
        out_specs=pl.BlockSpec((128, 48, 128), lambda g: (0, 0, 0)),
        out_shape=pltpu.HBM((128, 48, 128), BF16),
        scratch_shapes=[
            pltpu.VMEM((512, NLON // 2), BF16),
            pltpu.VMEM((16 * PAIRS, 128), F32),
        ],
        compiler_params=vmem(56),
        name="forward",
    )(in_vmem(x), table)


CHUNK = 128


def legendre_kernel(a_ref, b_ref, m_ref, cos_ref, start_ref, w_ref, ana_ref, syn_ref, rows, state):
    chunk = pl.program_id(0)
    upper = lax.broadcasted_iota(jnp.int32, (8, 128), 0) < 4

    @pl.when(chunk == 0)
    def _():
        state[...] = jnp.zeros_like(state)

    cosine = [cos_ref[8 * v:8 * v + 8, :] for v in range(3)]
    orders = [m_ref[8 * v:8 * v + 8, :] for v in range(3)]

    def body(it, carry):
        prev, curr, logs, scale = carry
        for k in range(4):
            local = it * 4 + k
            degree = chunk * CHUNK + local
            nxt = []
            new_logs = []
            new_scale = []
            for v in range(3):
                at = degree * 6 + 2 * v
                a = jnp.where(upper, a_ref[at], a_ref[at + 1])
                b = jnp.where(upper, b_ref[at], b_ref[at + 1])
                first = orders[v] == degree
                start = start_ref[8 * v:8 * v + 8, :]
                val = jnp.where(first, 1.0, (a * cosine[v]) * curr[v] - b * prev[v])
                lg = jnp.where(first, start, logs[v])
                sc = jnp.where(first, start_ref[24 + 8 * v:32 + 8 * v, :], scale[v])
                row = pl.multiple_of(local * 24, 8) + 8 * v
                rows[pl.ds(row, 8), :] = val * sc
                nxt.append(val)
                new_logs.append(lg)
                new_scale.append(sc)
            prev, curr, logs, scale = curr, nxt, new_logs, new_scale
        grow = [jnp.maximum(1.0, jnp.maximum(jnp.abs(p), jnp.abs(c))) for p, c in zip(prev, curr)]
        inv = [1.0 / g for g in grow]
        prev = [p * i for p, i in zip(prev, inv)]
        curr = [c * i for c, i in zip(curr, inv)]
        logs = [l + jnp.log(g) for l, g in zip(logs, grow)]
        scale = [jnp.where(s > -1.0, jnp.where(o <= chunk * CHUNK + it * 4 + 3, jnp.exp(l), 0.0), 0.0)
                 for s, l, o in zip(scale, logs, orders)]
        return prev, curr, logs, scale

    init = tuple([state[24 * n + 8 * v:24 * n + 8 * v + 8, :] for v in range(3)] for n in range(4))
    final = lax.fori_loop(0, CHUNK // 4, body, init)
    for n in range(4):
        for v in range(3):
            state[24 * n + 8 * v:24 * n + 8 * v + 8, :] = final[n][v]
    for o in range(6):
        for jb in range(4):
            val = rows[pl.ds(4 * o + jb, CHUNK, stride=24), :]
            syn_ref[o, :, 128 * jb:128 * jb + 128] = val.astype(BF16)
            ana_ref[o, :, 128 * jb:128 * jb + 128] = (val * w_ref[jb:jb + 1, :]).astype(BF16)


def legendre_tables(orders):
    half = NLAT // 2
    colatitude = math.pi * (jnp.arange(half, dtype=F32) + 0.5) / NLAT
    sine = jnp.sin(colatitude)
    order_f = orders.astype(F32)
    log_start = (
        -0.5 * math.log(2.0)
        + 0.5 * (lax.lgamma(order_f + 1.5) - gamma_three_halves - lax.lgamma(order_f + 1.0))
    )[:, None] + order_f[:, None] * jnp.log(sine)[None, :]
    log_start = log_start.reshape(24, 128)
    start = jnp.concatenate((log_start, jnp.exp(log_start)))
    cosine = jnp.tile(jnp.cos(colatitude).reshape(4, 128), (6, 1))
    weight = (sine * (math.pi / NLAT)).reshape(4, 128)
    deg = jnp.arange(ORDERS, dtype=F32)[:, None]
    running = orders[None, :] < jnp.arange(ORDERS, dtype=jnp.int32)[:, None]
    denom_a = jnp.maximum(deg * deg - order_f * order_f, 1.0)
    coef_a = jnp.where(running, jnp.sqrt(jnp.maximum(4.0 * deg * deg - 1.0, 0.0) / denom_a), 0.0)
    numer_b = jnp.maximum((deg - 1.0) * (deg - 1.0) - order_f * order_f, 0.0)
    denom_b = jnp.maximum(4.0 * (deg - 1.0) * (deg - 1.0) - 1.0, 1.0)
    coef_b = coef_a * jnp.sqrt(numer_b / denom_b)
    order_rows = jnp.broadcast_to(jnp.repeat(orders, 4)[:, None], (24, 128))
    smem = pl.BlockSpec(memory_space=pltpu.SMEM)
    full = pl.BlockSpec((24, 128), lambda g: (0, 0))
    return pl.pallas_call(
        legendre_kernel,
        grid=(ORDERS // CHUNK,),
        in_specs=[
            smem, smem, full, full,
            pl.BlockSpec((48, 128), lambda g: (0, 0)),
            pl.BlockSpec((4, 128), lambda g: (0, 0)),
        ],
        out_specs=[pl.BlockSpec((6, CHUNK, half), lambda g: (0, g, 0))] * 2,
        out_shape=[pltpu.HBM((6, ORDERS, half), BF16)] * 2,
        scratch_shapes=[pltpu.VMEM((CHUNK * 24, 128), F32), pltpu.VMEM((96, 128), F32)],
        name="legendre_tables",
    )(coef_a.reshape(-1), coef_b.reshape(-1), order_rows, cosine, start, weight)


def filter_kernel(slot_ref, ord_ref, f_ref, ana_ref, syn_ref, spec_ref, back_ref):
    sub = lax.broadcasted_iota(jnp.int32, (128, 128), 0)
    flip = jnp.where(sub + lane_ids((128, 128)) == 127, 1.0, 0.0).astype(BF16)
    for k in range(2):
        o = 2 * pl.program_id(0) + k
        order = ord_ref[o]
        plus = []
        minus = []
        for c in range(4):
            north = f_ref[c, :, o].astype(F32).reshape(128, 128)
            south = f_ref[7 - c, :, o].astype(F32).reshape(128, 128).astype(BF16)
            south = jnp.dot(south, flip, preferred_element_type=F32)
            plus.append((north + south).astype(BF16))
            minus.append((north - south).astype(BF16))
        both = jnp.concatenate(
            [jnp.concatenate(plus, axis=1), jnp.concatenate(minus, axis=1)], axis=0
        )
        coef = lax.dot_general(
            both, ana_ref[k], (((1,), (1,)), ((), ())), preferred_element_type=F32
        )
        even = ((lane_ids((128, ORDERS)) - order) & 1) == 0
        spec = jnp.where(even, coef[:128], coef[128:])
        spec_ref[slot_ref[o] & 1] = spec
        parts = jnp.concatenate([jnp.where(even, spec, 0.0), jnp.where(even, 0.0, spec)], axis=0)
        grid = jnp.dot(parts.astype(BF16), syn_ref[k], preferred_element_type=F32)
        factor = jnp.where(order == 0, 0.5, 1.0)
        north = (grid[:128] + grid[128:]) * factor
        south = ((grid[:128] - grid[128:]) * factor).astype(BF16)
        for c in range(4):
            cut = slice(128 * c, 128 * c + 128)
            back_ref[c, :, k] = north[:, cut].reshape(16, 8, 128).astype(BF16)
            turned = jnp.dot(south[:, cut], flip, preferred_element_type=F32)
            back_ref[7 - c, :, k] = turned.reshape(16, 8, 128).astype(BF16)


def legendre_filter(fourier, analysis, synthesis, orders, slots):
    table = pl.BlockSpec((2, ORDERS, NLAT // 2), lambda p, *_: (p, 0, 0))
    blocks = pl.BlockSpec((8, 16, 2, 8, 128), lambda p, *_: (0, 0, p, 0, 0))
    return pl.pallas_call(
        filter_kernel,
        grid_spec=pltpu.PrefetchScalarGridSpec(
            num_scalar_prefetch=2,
            grid=(3,),
            in_specs=[IN_VMEM, table, table],
            out_specs=[
                pl.BlockSpec((2, 128, ORDERS), lambda p, *_: (p, 0, 0)),
                blocks,
            ],
        ),
        out_shape=[
            pltpu.HBM((6, 128, ORDERS), F32),
            pltpu.HBM((8, 16, 6, 8, 128), BF16),
        ],
        compiler_params=vmem(56),
        name="legendre_filter",
    )(slots, orders, in_vmem(fourier), analysis, synthesis)


def inverse_kernel(y_ref, t_ref, o_ref, rows, cols):
    @pl.when(pl.program_id(0) == 0)
    def _():
        rows[...] = y_ref[...].astype(F32).reshape(rows.shape)
        for par in range(2):
            for ri in range(2):
                for a in range(4):
                    cols[par, PAIRS * ri:PAIRS * ri + PAIRS, 128 * a:128 * a + 128] = (
                        rows[pl.ds(8 * par + 2 * a + ri, PAIRS, stride=16), :].astype(BF16)
                    )

    width = NLON // 2 // 2
    sums = []
    for par in range(2):
        res = lax.dot_general(
            cols[par], t_ref[par].reshape(2 * PAIRS, width), (((0,), (0,)), ((), ())),
            preferred_element_type=F32,
        )
        sums.append(res * (2.0 / NLON))
    low = (sums[0] + sums[1]).astype(BF16)
    high = (sums[0] - sums[1]).astype(BF16)
    for b in range(width // 128):
        o_ref[0, b] = low[:, 128 * b:128 * b + 128].reshape(4, 128, 128)
        o_ref[1, b] = high[:, 128 * b:128 * b + 128].reshape(4, 128, 128)


def inverse(y, table):
    steps = 2
    width = NLON // 2 // steps
    out = pl.pallas_call(
        inverse_kernel,
        grid=(steps,),
        in_specs=[
            IN_VMEM,
            pl.BlockSpec((2, 2, PAIRS, width), lambda g: (0, 0, 0, g)),
        ],
        out_specs=pl.BlockSpec((2, width // 128, 4, 128, 128), lambda g: (0, g, 0, 0, 0)),
        out_shape=pltpu.HBM((2, 8, 4, 128, 128), BF16),
        scratch_shapes=[
            pltpu.VMEM((128 * 48, 128), F32),
            pltpu.VMEM((2, 2 * PAIRS, 512), BF16),
        ],
        compiler_params=vmem(56),
        name="inverse",
    )(in_vmem(y), table)
    return out.reshape(16, 4, 128, 128)


def update_kernel(se_ref, sp_ref, f_ref, old_ent, old_pres, oe_ref, op_ref):
    at = pl.ds(8 * pl.program_id(0), 8)
    oe_ref[...] = se_ref[...] + 0.5 * f_ref[0, at].astype(F32)
    op_ref[...] = sp_ref[...] + 0.5 * f_ref[1, at].astype(F32)


def update(start_entropy, start_pressure, filtered, ent, pres):
    whole = pl.BlockSpec((8, ROWS, COLS), lambda g: (g, 0, 0))
    anywhere = pl.BlockSpec(memory_space=pl.ANY)
    return pl.pallas_call(
        update_kernel,
        grid=(FLEV // 8,),
        in_specs=[whole, whole, IN_VMEM, anywhere, anywhere],
        out_specs=[whole, whole],
        out_shape=[pltpu.HBM((LEV, ROWS, COLS), F32)] * 2,
        input_output_aliases={3: 0, 4: 1},
        compiler_params=vmem(56),
        name="update",
    )(start_entropy, start_pressure, in_vmem(filtered), ent, pres)


def per_device(entropy, zonal_flux, meridional_flux, start_entropy, start_pressure, order_slot):
    n_lat = lax.axis_size("lat")
    n_lon = lax.axis_size("lonr")
    pairs = order_slot.reshape(PAIRS, 2)
    first_even = (pairs[:, 0] % 2) == 0
    even = jnp.where(first_even, pairs[:, 0], pairs[:, 1])
    odd = jnp.where(first_even, pairs[:, 1], pairs[:, 0])
    block = lax.axis_index("lat") * n_lon + lax.axis_index("lonr")
    both = jnp.stack((even, odd), axis=1)
    orders = lax.dynamic_slice_in_dim(both, block * 3, 3).reshape(6)
    swap = jnp.where(first_even, 0, 1).astype(jnp.int32)
    swap = lax.dynamic_slice_in_dim(swap, block * 3, 3)
    base = 2 * jnp.arange(3, dtype=jnp.int32)
    slots = jnp.stack((base + swap, base + 1 - swap), axis=1).reshape(6)

    first = (lax.axis_index("lat") * ROWS).astype(jnp.int32).reshape(1)
    east, west, south, north, fs, rc = edges(first, entropy, zonal_flux, meridional_flux)
    ring = range(n_lon)
    from_west = lax.ppermute(east, "lonr", [(i, (i + 1) % n_lon) for i in ring])
    from_east = lax.ppermute(west, "lonr", [((i + 1) % n_lon, i) for i in ring])
    from_north = lax.ppermute(south, "lat", [(i, i + 1) for i in range(n_lat - 1)])
    from_south = lax.ppermute(north, "lat", [(i + 1, i) for i in range(n_lat - 1)])
    table = fourier_table(jnp.stack((even, odd)))
    items, ent, pres = tendencies(
        entropy, zonal_flux, meridional_flux, from_west, from_east, west, from_north, from_south,
        fs, rc, start_entropy, start_pressure,
    )
    grid = lax.all_to_all(
        items.reshape(16, 4, ROWS, COLS), "lonr", split_axis=0, concat_axis=0, tiled=True
    )
    analysis, synthesis = legendre_tables(orders)
    spectral = forward(grid, table)
    spectral = lax.all_to_all(
        spectral, ("lat", "lonr"), split_axis=0, concat_axis=0, tiled=True
    )
    spectrum, back = legendre_filter(
        spectral.reshape(8, 16, 6, 8, 128), analysis, synthesis, orders, slots
    )
    back = lax.all_to_all(
        back.reshape(128, 48, 128), ("lat", "lonr"), split_axis=0, concat_axis=0, tiled=True
    )
    filtered = inverse(back, table)
    filtered = lax.all_to_all(filtered, "lonr", split_axis=0, concat_axis=0, tiled=True)
    new_entropy, new_pressure = update(
        start_entropy, start_pressure, filtered.reshape(2, FLEV, ROWS, COLS), ent, pres
    )
    return new_entropy, new_pressure, spectrum.reshape(6, 64, 2, ORDERS)


def solution(mesh):
    cube = P(None, "lat", "lonr")
    return jax.shard_map(
        per_device,
        mesh=mesh,
        in_specs=(cube, cube, cube, cube, cube, P()),
        out_specs=(cube, cube, P(("lat", "lonr"), None, None, None)),
        check_vma=False,
    )
```

```python
import math

import jax
import jax.numpy as jnp
from jax import lax
from jax.experimental import pallas as pl
from jax.experimental.pallas import tpu as pltpu
import numpy as np
from jax.sharding import PartitionSpec as P

FLEV = 32
LEV = 40
NLAT = 1024
NLON = 2048
ORDERS = 768
PAIRS = ORDERS // 2
ROWS = 128
COLS = 128
F32 = jnp.float32
BF16 = jnp.bfloat16

gamma_three_halves = 0.5 * math.log(math.pi) - math.log(2.0)


def vmem(mib):
    return pltpu.CompilerParams(vmem_limit_bytes=mib << 20)


IN_VMEM = pl.BlockSpec(memory_space=pltpu.VMEM)


def in_vmem(x):
    return pltpu.with_memory_space_constraint(x, pltpu.VMEM)


def lane_ids(shape):
    return lax.broadcasted_iota(jnp.int32, shape, len(shape) - 1)


def sine_of(n):
    x = jnp.minimum(n, NLAT - n) * (math.pi / NLAT)
    square = x * x
    total = jnp.full_like(x, 1.0 / math.factorial(13))
    for power in (11, 9, 7, 5, 3, 1):
        total = total * square + (-1.0) ** (power // 2) / math.factorial(power)
    return total * x


def edges_kernel(
    first_ref, s_any, u_any, v_ref, side_ref, south_ref, north_ref, fs_ref, rc_ref,
    s_ref, u_ref, sems
):
    lane = lane_ids((8, 128))
    owner = ((lane + 3) & 127) >> 3
    part = lane & 7
    parts = LEV // 8

    def fetch(n, g):
        at = pl.ds(8 * g, 8)
        src = (s_any, u_any)[n]
        dst = (s_ref, u_ref)[n]
        return pltpu.make_async_copy(src.at[at], dst.at[at], sems.at[n, g])

    for g in range(parts):
        for n in range(2):
            fetch(n, g).start()
    at = first_ref[0] - 8 + lax.broadcasted_iota(jnp.int32, (136, 128), 0)
    sines = sine_of((at + 1).astype(F32))
    fs_ref[...] = jnp.where((at >= 0) & (at < NLAT - 1), sines, 0.0)
    rc_ref[...] = 1.0 / sine_of(at[8:].astype(F32) + 0.5)

    def four_levels(q, carry):
        for k in range(4):
            lev = 4 * q + k
            side = jnp.zeros((8, 128), F32)
            flux = jnp.zeros((8, 128), F32)
            for i in range(16):
                s = s_ref[lev, pl.ds(8 * i, 8), :]
                u = u_ref[lev, pl.ds(8 * i, 8), :]
                side = jnp.where(owner == i, pltpu.roll(s, 8 * i, 1) if i else s, side)
                flux = jnp.where(owner == i, pltpu.roll(u, 8 * i, 1) if i else u, flux)
            side_ref[lev] = jnp.where(part == 4, pltpu.roll(flux, 125, 1), side)
            south_ref[lev, 0:3, :] = s_ref[lev, 125:128, :]
            north_ref[lev] = s_ref[lev, 0:4, :]
        return carry

    for g in range(parts):
        for n in range(2):
            fetch(n, g).wait()
        lax.fori_loop(2 * g, 2 * g + 2, four_levels, 0)
    for lev in range(LEV):
        south_ref[lev, 3:4, :] = v_ref[lev, 7:8, :]


def edges(first, entropy, zonal, merid):
    anywhere = pl.BlockSpec(memory_space=pl.ANY)
    return pl.pallas_call(
        edges_kernel,
        grid=(1,),
        in_specs=[pl.BlockSpec(memory_space=pltpu.SMEM), anywhere, anywhere, pl.BlockSpec((LEV, 8, COLS), lambda g: (0, ROWS // 8 - 1, 0))],
        out_specs=[pl.BlockSpec((LEV, n, 128), lambda g: (0, 0, 0)) for n in (8, 4, 4)]
        + [pl.BlockSpec((n, 128), lambda g: (0, 0)) for n in (136, 128)],
        out_shape=[
            pltpu.HBM((LEV, 8, 128), F32),
            pltpu.HBM((LEV, 4, 128), F32),
            pltpu.HBM((LEV, 4, 128), F32),
            pltpu.HBM((136, 128), F32),
            pltpu.HBM((128, 128), F32),
        ],
        scratch_shapes=[pltpu.VMEM((LEV, ROWS, COLS), F32)] * 2
        + [pltpu.SemaphoreType.DMA((2, LEV // 8))],
        name="edges",
    )(first, entropy, zonal, merid)


def stencil(x0, x1, x2, x3, x4, x5):
    return (37.0 * (x2 + x3) - 8.0 * (x1 + x4) + (x0 + x5)) * (1.0 / 60.0)


def stencil_matrices():
    weights = {-2: 1.0, -1: -8.0, 0: 37.0, 1: 37.0, 2: -8.0, 3: 1.0}
    along = np.zeros((256, 256), np.float32)
    across = np.zeros((128, 136), np.float32)
    for face in range(128):
        for shift, weight in weights.items():
            cell = face + shift
            along[cell if 0 <= cell < 128 else 128 + cell % 128 if cell >= 128 else 256 + cell, face] = weight
            across[face, cell if 0 <= cell < 128 else 128 + 4 + cell % 128 if cell >= 128 else 128 + 3 + cell] = weight
    along[128 + 3, 128 + 127] = 1.0
    along[128 + 124, 128] = 1.0
    return along, across


def split(x):
    high = x.astype(BF16)
    return high, (x - high.astype(F32)).astype(BF16)


def tend_kernel(
    s_ref, u_ref, v_ref, hw_ref, he_ref, ow_ref, hn_ref, hs_ref, fs_ref, rc_ref, along_ref, across_ref,
    se_ref, sp_ref, item_ref, ent_ref, pres_ref, cells, face, mext,
):
    step = pl.program_id(0)
    lane = lane_ids((ROWS, COLS))
    small = lane_ids((8, 128)) & 7
    across = across_ref[...]

    def prepare(lev):
        west = hw_ref[lev]
        own = ow_ref[lev]
        edge = stencil(
            pltpu.roll(west, 6, 1), pltpu.roll(west, 5, 1), pltpu.roll(west, 4, 1),
            pltpu.roll(own, 3, 1), pltpu.roll(own, 2, 1), pltpu.roll(own, 1, 1),
        )
        edge = edge * pltpu.roll(west, 7, 1)
        rim = jnp.where(small < 3, he_ref[lev], jnp.where(small == 3, edge, west))
        rim = jnp.concatenate([pltpu.roll(rim, (128 - 8 * i) % 128, 1) for i in range(16)])
        s = s_ref[lev]
        s_hi, s_lo = split(s)
        r_hi, r_lo = split(rim)
        at = slice(128 * lev, 128 * lev + 128)
        cells[at, 0:128] = s_hi
        cells[at, 128:256] = r_hi
        cells[at, 256:384] = s_lo
        cells[at, 384:512] = r_lo
        h_hi, h_lo = split(jnp.concatenate([hn_ref[lev], hs_ref[lev]]))
        face[lev, :, 256:384] = jnp.dot(
            across, jnp.concatenate([s_hi, s_lo, h_hi, h_lo]), preferred_element_type=F32
        )

    def multiply(part):
        rows = slice(512 * part, 512 * part + 512)
        res = jnp.dot(cells[rows, :], along_ref[...], preferred_element_type=F32)
        face[4 * part:4 * part + 4, :, 0:256] = res.reshape(4, 128, 256)

    def level(lev, put):
        half = lev % 4
        u = u_ref[lev]
        z = (u * (1.0 / 60.0)) * face[lev, :, 0:128]
        rim = face[lev, :, 128:256]
        dz = z - pltpu.roll(jnp.where(lane == COLS - 1, rim, z), 1, 1)
        du = u - jnp.where(lane == 0, rim, pltpu.roll(u, 1, 1))
        fv = v_ref[lev] * fs_ref[8:136, :]
        fv_top = hn_ref[lev, 3:4, :] * fs_ref[7:8, :]
        top = [hn_ref[lev, o:o + 1, :] for o in range(3)] + [s_ref[lev, o:o + 1, :] for o in range(3)]
        m = fv * (face[lev, :, 256:384] * (1.0 / 60.0))
        mext[half, 0, 7:8, :] = fv_top * stencil(*top)
        mext[half, 0, 8:136, :] = m
        mext[half, 1, 7:8, :] = fv_top
        mext[half, 1, 8:136, :] = fv
        rc = rc_ref[...]
        put(
            lev,
            -(dz + (m - mext[half, 0, 7:135, :]) * rc),
            -0.3 * (du + (fv - mext[half, 1, 7:135, :]) * rc),
        )

    def put_items(lev, ent, pres):
        item_ref[0, lev] = ent.astype(BF16)
        item_ref[1, lev] = pres.astype(BF16)

    def put_tail(lev, ent, pres):
        ent_ref[lev] = se_ref[lev] + 0.5 * ent
        pres_ref[lev] = sp_ref[lev] + 0.5 * pres

    def run(put):
        for lev in range(4):
            prepare(lev)
        multiply(0)
        for lev in range(4, 8):
            prepare(lev)
        multiply(1)
        for lev in range(8):
            level(lev, put)

    @pl.when(step < FLEV // 8)
    def _():
        run(put_items)

    @pl.when(step == FLEV // 8)
    def _():
        run(put_tail)


def tendencies(
    s, u, v, from_west, from_east, own_west, from_north, from_south, fs, rc, start_entropy, start_pressure
):
    whole = pl.BlockSpec((8, ROWS, COLS), lambda g: (g, 0, 0))
    packed = pl.BlockSpec((8, 8, 128), lambda g: (g, 0, 0))
    rows4 = pl.BlockSpec((8, 4, 128), lambda g: (g, 0, 0))
    tail = pl.BlockSpec((8, ROWS, COLS), lambda g: (FLEV // 8, 0, 0))
    along, across = stencil_matrices()
    along = jnp.asarray(np.concatenate((along, along)), BF16)
    across = np.concatenate(
        (across[:, :128], across[:, :128], across[:, 128:], across[:, 128:]), axis=1
    )
    return pl.pallas_call(
        tend_kernel,
        grid=(LEV // 8,),
        in_specs=[
            whole, whole, whole, packed, packed, packed, rows4, rows4,
            pl.BlockSpec((136, 128), lambda g: (0, 0)),
            pl.BlockSpec((128, 128), lambda g: (0, 0)),
            pl.BlockSpec((512, 256), lambda g: (0, 0)),
            pl.BlockSpec((128, 272), lambda g: (0, 0)),
            tail, tail,
        ],
        out_specs=[
            pl.BlockSpec((2, 8, ROWS, COLS), lambda g: (0, jnp.minimum(g, FLEV // 8 - 1), 0, 0)),
            tail, tail,
        ],
        out_shape=[
            pltpu.HBM((2, FLEV, ROWS, COLS), BF16),
            pltpu.HBM((LEV, ROWS, COLS), F32),
            pltpu.HBM((LEV, ROWS, COLS), F32),
        ],
        scratch_shapes=[
            pltpu.VMEM((1024, 512), BF16),
            pltpu.VMEM((8, 128, 384), F32),
            pltpu.VMEM((4, 2, 136, 128), F32),
        ],
        name="tendencies",
    )(s, u, v, from_west, from_east, own_west, from_north, from_south, fs, rc,
      along, jnp.asarray(across, BF16), start_entropy, start_pressure)


def table_kernel(base_ref, turn_ref, out_ref):
    for par in range(2):
        c = base_ref[par, 0]
        s = base_ref[par, 1]
        for b in range(8):
            tc = jnp.broadcast_to(turn_ref[par, :, b:b + 1], c.shape)
            ts = jnp.broadcast_to(turn_ref[par, :, 8 + b:9 + b], c.shape)
            out_ref[par, 0, :, 128 * b:128 * b + 128] = (c * tc - s * ts).astype(BF16)
            out_ref[par, 1, :, 128 * b:128 * b + 128] = (s * tc + c * ts).astype(BF16)


def fourier_table(even_odd):
    def angles(steps):
        product = (even_odd[:, :, None] * steps[None, None, :]) % NLON
        return (2.0 * math.pi / NLON) * product.astype(F32)

    near = angles(jnp.arange(128, dtype=jnp.int32))
    far = angles(128 * jnp.arange(8, dtype=jnp.int32))
    base = jnp.stack((jnp.cos(near), jnp.sin(near)), axis=1)
    turn = jnp.concatenate((jnp.cos(far), jnp.sin(far)), axis=2)
    tile = 96
    return pl.pallas_call(
        table_kernel,
        grid=(PAIRS // tile,),
        in_specs=[
            pl.BlockSpec((2, 2, tile, 128), lambda g: (0, 0, g, 0)),
            pl.BlockSpec((2, tile, 16), lambda g: (0, g, 0)),
        ],
        out_specs=pl.BlockSpec((2, 2, tile, NLON // 2), lambda g: (0, 0, g, 0)),
        out_shape=pltpu.HBM((2, 2, PAIRS, NLON // 2), BF16),
        name="longitude_table",
    )(base, turn)


def forward_kernel(x_ref, t_any, o_ref, fold, rows, t_ref, sems):
    par = pl.program_id(0)

    def fetch(n):
        return pltpu.make_async_copy(t_any.at[n], t_ref.at[n], sems.at[n])

    @pl.when(par == 0)
    def _():
        fetch(0).start()
        fetch(1).start()

    for a in range(4):
        for b in range(8):
            lo = x_ref[b, a]
            hi = x_ref[b + 8, a]
            fold[128 * a:128 * a + 128, 128 * b:128 * b + 128] = lo + jnp.where(par == 0, hi, -hi)
    fetch(par).wait()
    res = lax.dot_general(
        t_ref[par].reshape(2 * PAIRS, NLON // 2), fold[...], (((1,), (1,)), ((), ())),
        preferred_element_type=F32,
    )
    for ri in range(2):
        for a in range(4):
            rows[pl.ds(8 * par + 2 * a + ri, PAIRS, stride=16), :] = (
                res[PAIRS * ri:PAIRS * ri + PAIRS, 128 * a:128 * a + 128]
            )

    @pl.when(par == 1)
    def _():
        o_ref[...] = rows[...].reshape(o_ref.shape).astype(BF16)


def forward(x, table):
    return pl.pallas_call(
        forward_kernel,
        grid=(2,),
        in_specs=[
            IN_VMEM,
            pl.BlockSpec(memory_space=pl.ANY),
        ],
        out_specs=pl.BlockSpec((128, 48, 128), lambda g: (0, 0, 0)),
        out_shape=pltpu.HBM((128, 48, 128), BF16),
        scratch_shapes=[
            pltpu.VMEM((512, NLON // 2), BF16),
            pltpu.VMEM((16 * PAIRS, 128), F32),
            pltpu.VMEM((2, 2, PAIRS, NLON // 2), BF16),
            pltpu.SemaphoreType.DMA((2,)),
        ],
        compiler_params=vmem(56),
        name="forward",
    )(in_vmem(x), table)


CHUNK = 128


def legendre_kernel(a_ref, b_ref, m_ref, cos_ref, start_ref, w_ref, ana_ref, syn_ref, rows, state):
    chunk = pl.program_id(0)
    upper = lax.broadcasted_iota(jnp.int32, (8, 128), 0) < 4

    @pl.when(chunk == 0)
    def _():
        state[...] = jnp.zeros_like(state)

    cosine = [cos_ref[8 * v:8 * v + 8, :] for v in range(3)]
    orders = [m_ref[8 * v:8 * v + 8, :] for v in range(3)]

    def body(it, carry):
        prev, curr, logs, scale = carry
        for k in range(4):
            local = it * 4 + k
            degree = chunk * CHUNK + local
            nxt = []
            new_logs = []
            new_scale = []
            for v in range(3):
                at = degree * 6 + 2 * v
                a = jnp.where(upper, a_ref[at], a_ref[at + 1])
                b = jnp.where(upper, b_ref[at], b_ref[at + 1])
                first = orders[v] == degree
                start = start_ref[8 * v:8 * v + 8, :]
                val = jnp.where(first, 1.0, (a * cosine[v]) * curr[v] - b * prev[v])
                lg = jnp.where(first, start, logs[v])
                sc = jnp.where(first, start_ref[24 + 8 * v:32 + 8 * v, :], scale[v])
                row = pl.multiple_of(local * 24, 8) + 8 * v
                rows[pl.ds(row, 8), :] = val * sc
                nxt.append(val)
                new_logs.append(lg)
                new_scale.append(sc)
            prev, curr, logs, scale = curr, nxt, new_logs, new_scale
        grow = [jnp.maximum(1.0, jnp.maximum(jnp.abs(p), jnp.abs(c))) for p, c in zip(prev, curr)]
        inv = [1.0 / g for g in grow]
        prev = [p * i for p, i in zip(prev, inv)]
        curr = [c * i for c, i in zip(curr, inv)]
        logs = [l + jnp.log(g) for l, g in zip(logs, grow)]
        scale = [jnp.where(s > -1.0, jnp.where(o <= chunk * CHUNK + it * 4 + 3, jnp.exp(l), 0.0), 0.0)
                 for s, l, o in zip(scale, logs, orders)]
        return prev, curr, logs, scale

    init = tuple([state[24 * n + 8 * v:24 * n + 8 * v + 8, :] for v in range(3)] for n in range(4))
    final = lax.fori_loop(0, CHUNK // 4, body, init)
    for n in range(4):
        for v in range(3):
            state[24 * n + 8 * v:24 * n + 8 * v + 8, :] = final[n][v]
    for o in range(6):
        for jb in range(4):
            val = rows[pl.ds(4 * o + jb, CHUNK, stride=24), :]
            syn_ref[o, :, 128 * jb:128 * jb + 128] = val.astype(BF16)
            ana_ref[o, :, 128 * jb:128 * jb + 128] = (val * w_ref[jb:jb + 1, :]).astype(BF16)


def legendre_tables(orders):
    half = NLAT // 2
    colatitude = math.pi * (jnp.arange(half, dtype=F32) + 0.5) / NLAT
    sine = jnp.sin(colatitude)
    order_f = orders.astype(F32)
    log_start = (
        -0.5 * math.log(2.0)
        + 0.5 * (lax.lgamma(order_f + 1.5) - gamma_three_halves - lax.lgamma(order_f + 1.0))
    )[:, None] + order_f[:, None] * jnp.log(sine)[None, :]
    log_start = log_start.reshape(24, 128)
    start = jnp.concatenate((log_start, jnp.exp(log_start)))
    cosine = jnp.tile(jnp.cos(colatitude).reshape(4, 128), (6, 1))
    weight = (sine * (math.pi / NLAT)).reshape(4, 128)
    deg = jnp.arange(ORDERS, dtype=F32)[:, None]
    running = orders[None, :] < jnp.arange(ORDERS, dtype=jnp.int32)[:, None]
    denom_a = jnp.maximum(deg * deg - order_f * order_f, 1.0)
    coef_a = jnp.where(running, jnp.sqrt(jnp.maximum(4.0 * deg * deg - 1.0, 0.0) / denom_a), 0.0)
    numer_b = jnp.maximum((deg - 1.0) * (deg - 1.0) - order_f * order_f, 0.0)
    denom_b = jnp.maximum(4.0 * (deg - 1.0) * (deg - 1.0) - 1.0, 1.0)
    coef_b = coef_a * jnp.sqrt(numer_b / denom_b)
    order_rows = jnp.broadcast_to(jnp.repeat(orders, 4)[:, None], (24, 128))
    smem = pl.BlockSpec(memory_space=pltpu.SMEM)
    full = pl.BlockSpec((24, 128), lambda g: (0, 0))
    return pl.pallas_call(
        legendre_kernel,
        grid=(ORDERS // CHUNK,),
        in_specs=[
            smem, smem, full, full,
            pl.BlockSpec((48, 128), lambda g: (0, 0)),
            pl.BlockSpec((4, 128), lambda g: (0, 0)),
        ],
        out_specs=[pl.BlockSpec((6, CHUNK, half), lambda g: (0, g, 0))] * 2,
        out_shape=[pltpu.HBM((6, ORDERS, half), BF16)] * 2,
        scratch_shapes=[pltpu.VMEM((CHUNK * 24, 128), F32), pltpu.VMEM((96, 128), F32)],
        name="legendre_tables",
    )(coef_a.reshape(-1), coef_b.reshape(-1), order_rows, cosine, start, weight)


def filter_kernel(slot_ref, ord_ref, f_ref, ana_ref, syn_ref, spec_ref, back_ref):
    sub = lax.broadcasted_iota(jnp.int32, (128, 128), 0)
    flip = jnp.where(sub + lane_ids((128, 128)) == 127, 1.0, 0.0).astype(BF16)
    for k in range(2):
        o = 2 * pl.program_id(0) + k
        order = ord_ref[o]
        plus = []
        minus = []
        for c in range(4):
            north = f_ref[c, :, o].astype(F32).reshape(128, 128)
            south = f_ref[7 - c, :, o].astype(F32).reshape(128, 128).astype(BF16)
            south = jnp.dot(south, flip, preferred_element_type=F32)
            plus.append((north + south).astype(BF16))
            minus.append((north - south).astype(BF16))
        both = jnp.concatenate(
            [jnp.concatenate(plus, axis=1), jnp.concatenate(minus, axis=1)], axis=0
        )
        coef = lax.dot_general(
            both, ana_ref[k], (((1,), (1,)), ((), ())), preferred_element_type=F32
        )
        even = ((lane_ids((128, ORDERS)) - order) & 1) == 0
        spec = jnp.where(even, coef[:128], coef[128:])
        spec_ref[slot_ref[o] & 1] = spec
        parts = jnp.concatenate([jnp.where(even, spec, 0.0), jnp.where(even, 0.0, spec)], axis=0)
        grid = jnp.dot(parts.astype(BF16), syn_ref[k], preferred_element_type=F32)
        factor = jnp.where(order == 0, 0.5, 1.0)
        north = (grid[:128] + grid[128:]) * factor
        south = ((grid[:128] - grid[128:]) * factor).astype(BF16)
        for c in range(4):
            cut = slice(128 * c, 128 * c + 128)
            back_ref[c, :, k] = north[:, cut].reshape(16, 8, 128).astype(BF16)
            turned = jnp.dot(south[:, cut], flip, preferred_element_type=F32)
            back_ref[7 - c, :, k] = turned.reshape(16, 8, 128).astype(BF16)


def legendre_filter(fourier, analysis, synthesis, orders, slots):
    table = pl.BlockSpec((2, ORDERS, NLAT // 2), lambda p, *_: (p, 0, 0))
    blocks = pl.BlockSpec((8, 16, 2, 8, 128), lambda p, *_: (0, 0, p, 0, 0))
    return pl.pallas_call(
        filter_kernel,
        grid_spec=pltpu.PrefetchScalarGridSpec(
            num_scalar_prefetch=2,
            grid=(3,),
            in_specs=[IN_VMEM, table, table],
            out_specs=[
                pl.BlockSpec((2, 128, ORDERS), lambda p, *_: (p, 0, 0)),
                blocks,
            ],
        ),
        out_shape=[
            pltpu.HBM((6, 128, ORDERS), F32),
            pltpu.HBM((8, 16, 6, 8, 128), BF16),
        ],
        compiler_params=vmem(56),
        name="legendre_filter",
    )(slots, orders, in_vmem(fourier), analysis, synthesis)


def inverse_kernel(y_ref, t_any, o_ref, rows, cols, t_ref, sems):
    step = pl.program_id(0)
    width = NLON // 2 // 2

    def fetch(n, par):
        at = pl.ds(pl.multiple_of(n * width, width), width)
        return pltpu.make_async_copy(
            t_any.at[par, :, :, at], t_ref.at[n, par], sems.at[n, par]
        )

    @pl.when(step == 0)
    def _():
        for n in range(2):
            for par in range(2):
                fetch(n, par).start()
        rows[...] = y_ref[...].astype(F32).reshape(rows.shape)
        for par in range(2):
            for ri in range(2):
                for a in range(4):
                    cols[par, PAIRS * ri:PAIRS * ri + PAIRS, 128 * a:128 * a + 128] = (
                        rows[pl.ds(8 * par + 2 * a + ri, PAIRS, stride=16), :].astype(BF16)
                    )

    sums = []
    for par in range(2):
        fetch(step, par).wait()
        res = lax.dot_general(
            cols[par], t_ref[step, par].reshape(2 * PAIRS, width), (((0,), (0,)), ((), ())),
            preferred_element_type=F32,
        )
        sums.append(res * (2.0 / NLON))
    low = (sums[0] + sums[1]).astype(BF16)
    high = (sums[0] - sums[1]).astype(BF16)
    for b in range(width // 128):
        o_ref[0, b] = low[:, 128 * b:128 * b + 128].reshape(4, 128, 128)
        o_ref[1, b] = high[:, 128 * b:128 * b + 128].reshape(4, 128, 128)


def inverse(y, table):
    steps = 2
    width = NLON // 2 // steps
    out = pl.pallas_call(
        inverse_kernel,
        grid=(steps,),
        in_specs=[
            IN_VMEM,
            pl.BlockSpec(memory_space=pl.ANY),
        ],
        out_specs=pl.BlockSpec((2, width // 128, 4, 128, 128), lambda g: (0, g, 0, 0, 0)),
        out_shape=pltpu.HBM((2, 8, 4, 128, 128), BF16),
        scratch_shapes=[
            pltpu.VMEM((128 * 48, 128), F32),
            pltpu.VMEM((2, 2 * PAIRS, 512), BF16),
            pltpu.VMEM((steps, 2, 2, PAIRS, width), BF16),
            pltpu.SemaphoreType.DMA((steps, 2)),
        ],
        compiler_params=vmem(56),
        name="inverse",
    )(in_vmem(y), table)
    return out.reshape(16, 4, 128, 128)


def update_kernel(se_ref, sp_ref, f_ref, old_ent, old_pres, oe_ref, op_ref):
    at = pl.ds(8 * pl.program_id(0), 8)
    oe_ref[...] = se_ref[...] + 0.5 * f_ref[0, at].astype(F32)
    op_ref[...] = sp_ref[...] + 0.5 * f_ref[1, at].astype(F32)


def update(start_entropy, start_pressure, filtered, ent, pres):
    whole = pl.BlockSpec((8, ROWS, COLS), lambda g: (g, 0, 0))
    anywhere = pl.BlockSpec(memory_space=pl.ANY)
    return pl.pallas_call(
        update_kernel,
        grid=(FLEV // 8,),
        in_specs=[whole, whole, IN_VMEM, anywhere, anywhere],
        out_specs=[whole, whole],
        out_shape=[pltpu.HBM((LEV, ROWS, COLS), F32)] * 2,
        input_output_aliases={3: 0, 4: 1},
        compiler_params=vmem(56),
        name="update",
    )(start_entropy, start_pressure, in_vmem(filtered), ent, pres)


def per_device(entropy, zonal_flux, meridional_flux, start_entropy, start_pressure, order_slot):
    n_lat = lax.axis_size("lat")
    n_lon = lax.axis_size("lonr")
    pairs = order_slot.reshape(PAIRS, 2)
    first_even = (pairs[:, 0] % 2) == 0
    even = jnp.where(first_even, pairs[:, 0], pairs[:, 1])
    odd = jnp.where(first_even, pairs[:, 1], pairs[:, 0])
    block = lax.axis_index("lat") * n_lon + lax.axis_index("lonr")
    both = jnp.stack((even, odd), axis=1)
    orders = lax.dynamic_slice_in_dim(both, block * 3, 3).reshape(6)
    swap = jnp.where(first_even, 0, 1).astype(jnp.int32)
    swap = lax.dynamic_slice_in_dim(swap, block * 3, 3)
    base = 2 * jnp.arange(3, dtype=jnp.int32)
    slots = jnp.stack((base + swap, base + 1 - swap), axis=1).reshape(6)

    first = (lax.axis_index("lat") * ROWS).astype(jnp.int32).reshape(1)
    side, south, north, fs, rc = edges(first, entropy, zonal_flux, meridional_flux)
    ring = range(n_lon)
    from_west = lax.ppermute(side, "lonr", [(i, (i + 1) % n_lon) for i in ring])
    from_east = lax.ppermute(side, "lonr", [((i + 1) % n_lon, i) for i in ring])
    from_north = lax.ppermute(south, "lat", [(i, i + 1) for i in range(n_lat - 1)])
    from_south = lax.ppermute(north, "lat", [(i + 1, i) for i in range(n_lat - 1)])
    table = fourier_table(jnp.stack((even, odd)))
    items, ent, pres = tendencies(
        entropy, zonal_flux, meridional_flux, from_west, from_east, side, from_north, from_south,
        fs, rc, start_entropy, start_pressure,
    )
    grid = lax.all_to_all(
        items.reshape(16, 4, ROWS, COLS), "lonr", split_axis=0, concat_axis=0, tiled=True
    )
    analysis, synthesis = legendre_tables(orders)
    spectral = forward(grid, table)
    spectral = lax.all_to_all(
        spectral, ("lat", "lonr"), split_axis=0, concat_axis=0, tiled=True
    )
    spectrum, back = legendre_filter(
        spectral.reshape(8, 16, 6, 8, 128), analysis, synthesis, orders, slots
    )
    back = lax.all_to_all(
        back.reshape(128, 48, 128), ("lat", "lonr"), split_axis=0, concat_axis=0, tiled=True
    )
    filtered = inverse(back, table)
    filtered = lax.all_to_all(filtered, "lonr", split_axis=0, concat_axis=0, tiled=True)
    new_entropy, new_pressure = update(
        start_entropy, start_pressure, filtered.reshape(2, FLEV, ROWS, COLS), ent, pres
    )
    return new_entropy, new_pressure, spectrum.reshape(6, 64, 2, ORDERS)


def solution(mesh):
    cube = P(None, "lat", "lonr")
    return jax.shard_map(
        per_device,
        mesh=mesh,
        in_specs=(cube, cube, cube, cube, cube, P()),
        out_specs=(cube, cube, P(("lat", "lonr"), None, None, None)),
        check_vma=False,
    )
```

```python
import functools
import math

import jax
import jax.numpy as jnp
from jax import lax
from jax.experimental import pallas as pl
from jax.experimental.pallas import tpu as pltpu
import numpy as np
from jax.sharding import PartitionSpec as P

FLEV = 32
LEV = 40
NLAT = 1024
NLON = 2048
ORDERS = 768
PAIRS = ORDERS // 2
ROWS = 128
COLS = 128
F32 = jnp.float32
BF16 = jnp.bfloat16

gamma_three_halves = 0.5 * math.log(math.pi) - math.log(2.0)


def vmem(mib):
    return pltpu.CompilerParams(vmem_limit_bytes=mib << 20)


IN_VMEM = pl.BlockSpec(memory_space=pltpu.VMEM)


def in_vmem(x):
    return pltpu.with_memory_space_constraint(x, pltpu.VMEM)


def lane_ids(shape):
    return lax.broadcasted_iota(jnp.int32, shape, len(shape) - 1)


def sine_of(n):
    x = jnp.minimum(n, NLAT - n) * (math.pi / NLAT)
    square = x * x
    total = jnp.full_like(x, 1.0 / math.factorial(13))
    for power in (11, 9, 7, 5, 3, 1):
        total = total * square + (-1.0) ** (power // 2) / math.factorial(power)
    return total * x


def edges_kernel(
    first_ref, s_any, u_any, v_ref, side_ref, south_ref, north_ref, fs_ref, rc_ref,
    s_ref, u_ref, sems
):
    lane = lane_ids((8, 128))
    owner = ((lane + 3) & 127) >> 3
    part = lane & 7
    parts = LEV // 8

    def fetch(n, g):
        at = pl.ds(8 * g, 8)
        src = (s_any, u_any)[n]
        dst = (s_ref, u_ref)[n]
        return pltpu.make_async_copy(src.at[at], dst.at[at], sems.at[n, g])

    for g in range(parts):
        for n in range(2):
            fetch(n, g).start()
    at = first_ref[0] - 8 + lax.broadcasted_iota(jnp.int32, (136, 128), 0)
    sines = sine_of((at + 1).astype(F32))
    fs_ref[...] = jnp.where((at >= 0) & (at < NLAT - 1), sines, 0.0)
    rc_ref[...] = 1.0 / sine_of(at[8:].astype(F32) + 0.5)

    def four_levels(q, carry):
        for k in range(4):
            lev = 4 * q + k
            side = jnp.zeros((8, 128), F32)
            flux = jnp.zeros((8, 128), F32)
            for i in range(16):
                s = s_ref[lev, pl.ds(8 * i, 8), :]
                u = u_ref[lev, pl.ds(8 * i, 8), :]
                side = jnp.where(owner == i, pltpu.roll(s, 8 * i, 1) if i else s, side)
                flux = jnp.where(owner == i, pltpu.roll(u, 8 * i, 1) if i else u, flux)
            side_ref[lev] = jnp.where(part == 4, pltpu.roll(flux, 125, 1), side)
            south_ref[lev, 0:3, :] = s_ref[lev, 125:128, :]
            north_ref[lev] = s_ref[lev, 0:4, :]
        return carry

    for g in range(parts):
        for n in range(2):
            fetch(n, g).wait()
        lax.fori_loop(2 * g, 2 * g + 2, four_levels, 0)
    for lev in range(LEV):
        south_ref[lev, 3:4, :] = v_ref[lev, 7:8, :]


def edges(first, entropy, zonal, merid):
    anywhere = pl.BlockSpec(memory_space=pl.ANY)
    return pl.pallas_call(
        edges_kernel,
        grid=(1,),
        in_specs=[pl.BlockSpec(memory_space=pltpu.SMEM), anywhere, anywhere, pl.BlockSpec((LEV, 8, COLS), lambda g: (0, ROWS // 8 - 1, 0))],
        out_specs=[pl.BlockSpec((LEV, n, 128), lambda g: (0, 0, 0)) for n in (8, 4, 4)]
        + [pl.BlockSpec((n, 128), lambda g: (0, 0)) for n in (136, 128)],
        out_shape=[
            pltpu.HBM((LEV, 8, 128), F32),
            pltpu.HBM((LEV, 4, 128), F32),
            pltpu.HBM((LEV, 4, 128), F32),
            pltpu.HBM((136, 128), F32),
            pltpu.HBM((128, 128), F32),
        ],
        scratch_shapes=[pltpu.VMEM((LEV, ROWS, COLS), F32)] * 2
        + [pltpu.SemaphoreType.DMA((2, LEV // 8))],
        name="edges",
    )(first, entropy, zonal, merid)


def stencil(x0, x1, x2, x3, x4, x5):
    return (37.0 * (x2 + x3) - 8.0 * (x1 + x4) + (x0 + x5)) * (1.0 / 60.0)


def stencil_matrices():
    weights = {-2: 1.0, -1: -8.0, 0: 37.0, 1: 37.0, 2: -8.0, 3: 1.0}
    along = np.zeros((256, 256), np.float32)
    across = np.zeros((128, 136), np.float32)
    for face in range(128):
        for shift, weight in weights.items():
            cell = face + shift
            along[cell if 0 <= cell < 128 else 128 + cell % 128 if cell >= 128 else 256 + cell, face] = weight
            across[face, cell if 0 <= cell < 128 else 128 + 4 + cell % 128 if cell >= 128 else 128 + 3 + cell] = weight
    along[128 + 3, 128 + 127] = 1.0
    along[128 + 124, 128] = 1.0
    return along, across


def split(x):
    high = x.astype(BF16)
    return high, (x - high.astype(F32)).astype(BF16)


def tend_kernel(*refs):
    (s_ref, u_ref, v_ref, hw_ref, he_ref, ow_ref, hn_ref, hs_ref, fs_ref, rc_ref, along_ref,
     across_ref) = refs[:12]
    cells, face, mext = refs[-3:]
    wide = s_ref.shape[1]
    lane = lane_ids((ROWS, COLS))
    small = lane_ids((8, 128)) & 7
    across = across_ref[...]

    def prepare(lev):
        west = hw_ref[lev // wide, lev % wide]
        own = ow_ref[lev // wide, lev % wide]
        edge = stencil(
            pltpu.roll(west, 6, 1), pltpu.roll(west, 5, 1), pltpu.roll(west, 4, 1),
            pltpu.roll(own, 3, 1), pltpu.roll(own, 2, 1), pltpu.roll(own, 1, 1),
        )
        edge = edge * pltpu.roll(west, 7, 1)
        rim = jnp.where(small < 3, he_ref[lev // wide, lev % wide], jnp.where(small == 3, edge, west))
        rim = jnp.concatenate([pltpu.roll(rim, (128 - 8 * i) % 128, 1) for i in range(16)])
        s = s_ref[lev // wide, lev % wide]
        s_hi, s_lo = split(s)
        r_hi, r_lo = split(rim)
        at = slice(128 * lev, 128 * lev + 128)
        cells[at, 0:128] = s_hi
        cells[at, 128:256] = r_hi
        cells[at, 256:384] = s_lo
        cells[at, 384:512] = r_lo
        h_hi, h_lo = split(jnp.concatenate([hn_ref[lev // wide, lev % wide], hs_ref[lev // wide, lev % wide]]))
        face[lev, :, 256:384] = jnp.dot(
            across, jnp.concatenate([s_hi, s_lo, h_hi, h_lo]), preferred_element_type=F32
        )

    def multiply(part):
        rows = slice(512 * part, 512 * part + 512)
        res = jnp.dot(cells[rows, :], along_ref[...], preferred_element_type=F32)
        face[4 * part:4 * part + 4, :, 0:256] = res.reshape(4, 128, 256)

    def level(lev):
        half = lev % 4
        u = u_ref[lev // wide, lev % wide]
        z = (u * (1.0 / 60.0)) * face[lev, :, 0:128]
        rim = face[lev, :, 128:256]
        dz = z - pltpu.roll(jnp.where(lane == COLS - 1, rim, z), 1, 1)
        du = u - jnp.where(lane == 0, rim, pltpu.roll(u, 1, 1))
        fv = v_ref[lev // wide, lev % wide] * fs_ref[8:136, :]
        fv_top = hn_ref[lev // wide, lev % wide, 3:4, :] * fs_ref[7:8, :]
        top = [hn_ref[lev // wide, lev % wide, o:o + 1, :] for o in range(3)] + [s_ref[lev // wide, lev % wide, o:o + 1, :] for o in range(3)]
        m = fv * (face[lev, :, 256:384] * (1.0 / 60.0))
        mext[half, 0, 7:8, :] = fv_top * stencil(*top)
        mext[half, 0, 8:136, :] = m
        mext[half, 1, 7:8, :] = fv_top
        mext[half, 1, 8:136, :] = fv
        rc = rc_ref[...]
        ent = -(dz + (m - mext[half, 0, 7:135, :]) * rc)
        pres = -0.3 * (du + (fv - mext[half, 1, 7:135, :]) * rc)
        return ent, pres

    def put(lev, ent, pres):
        if len(refs) == 16:
            item_ref = refs[12]
            item_ref[0, lev // 2, lev % 2] = ent.astype(BF16)
            item_ref[1, lev // 2, lev % 2] = pres.astype(BF16)
        else:
            se_ref, sp_ref, ent_ref, pres_ref = refs[12:16]
            ent_ref[lev] = se_ref[lev] + 0.5 * ent
            pres_ref[lev] = sp_ref[lev] + 0.5 * pres

    for lev in range(4):
        prepare(lev)
    multiply(0)
    for lev in range(4, 8):
        prepare(lev)
    multiply(1)
    for lev in range(8):
        put(lev, *level(lev))


def tendencies(fields, halos, factors, starts=None, half=None):
    groups = LEV // 4
    if half is None:
        deep, wide, steps = 2, 4, 1

        def at(g):
            return (FLEV // 8, 0)
    else:
        deep, wide, steps = 4, 2, 2

        def at(g):
            return (g, half)

    def spec(rows):
        return pl.BlockSpec((deep, wide, rows, 128), lambda g: at(g) + (0, 0))

    along, across = stencil_matrices()
    along = jnp.asarray(np.concatenate((along, along)), BF16)
    across = np.concatenate(
        (across[:, :128], across[:, :128], across[:, 128:], across[:, 128:]), axis=1
    )
    operands = [x.reshape(groups, 4, *x.shape[1:]) for x in (*fields, *halos)]
    in_specs = [spec(x.shape[2]) for x in operands]
    operands += [*factors, along, jnp.asarray(across, BF16)]
    in_specs += [
        pl.BlockSpec((136, 128), lambda g: (0, 0)),
        pl.BlockSpec((128, 128), lambda g: (0, 0)),
        pl.BlockSpec((512, 256), lambda g: (0, 0)),
        pl.BlockSpec((128, 272), lambda g: (0, 0)),
    ]
    if half is None:
        tail = pl.BlockSpec((8, ROWS, COLS), lambda g: (FLEV // 8, 0, 0))
        operands += starts
        in_specs += [tail, tail]
        out_specs = [tail, tail]
        out_shape = [pltpu.HBM((LEV, ROWS, COLS), F32)] * 2
    else:
        out_specs = pl.BlockSpec((2, 4, 2, ROWS, COLS), lambda g: (0, g, 0, 0, 0))
        out_shape = pltpu.HBM((2, 8, 2, ROWS, COLS), BF16)
    return pl.pallas_call(
        tend_kernel,
        grid=(steps,),
        in_specs=in_specs,
        out_specs=out_specs,
        out_shape=out_shape,
        scratch_shapes=[
            pltpu.VMEM((1024, 512), BF16),
            pltpu.VMEM((8, 128, 384), F32),
            pltpu.VMEM((4, 2, 136, 128), F32),
        ],
        name="tendencies" if half is not None else "tail",
    )(*operands)


def table_kernel(base_ref, turn_ref, out_ref):
    for par in range(2):
        c = base_ref[par, 0]
        s = base_ref[par, 1]
        for b in range(8):
            tc = jnp.broadcast_to(turn_ref[par, :, b:b + 1], c.shape)
            ts = jnp.broadcast_to(turn_ref[par, :, 8 + b:9 + b], c.shape)
            out_ref[par, 0, :, 128 * b:128 * b + 128] = (c * tc - s * ts).astype(BF16)
            out_ref[par, 1, :, 128 * b:128 * b + 128] = (s * tc + c * ts).astype(BF16)


def fourier_table(even_odd):
    def angles(steps):
        product = (even_odd[:, :, None] * steps[None, None, :]) % NLON
        return (2.0 * math.pi / NLON) * product.astype(F32)

    near = angles(jnp.arange(128, dtype=jnp.int32))
    far = angles(128 * jnp.arange(8, dtype=jnp.int32))
    base = jnp.stack((jnp.cos(near), jnp.sin(near)), axis=1)
    turn = jnp.concatenate((jnp.cos(far), jnp.sin(far)), axis=2)
    tile = 96
    return pl.pallas_call(
        table_kernel,
        grid=(PAIRS // tile,),
        in_specs=[
            pl.BlockSpec((2, 2, tile, 128), lambda g: (0, 0, g, 0)),
            pl.BlockSpec((2, tile, 16), lambda g: (0, g, 0)),
        ],
        out_specs=pl.BlockSpec((2, 2, tile, NLON // 2), lambda g: (0, 0, g, 0)),
        out_shape=pltpu.HBM((2, 2, PAIRS, NLON // 2), BF16),
        name="longitude_table",
    )(base, turn)


def forward_kernel(half, *refs):
    if half == 0:
        x_ref, t_any, rows, fold, t_ref, sems = refs
    else:
        x_ref, t_any, r_any, o_ref, fold, t_ref, sems, rows = refs
    par = pl.program_id(0)

    def fetch(n):
        return pltpu.make_async_copy(t_any.at[n], t_ref.at[n], sems.at[n])

    @pl.when(par == 0)
    def _():
        fetch(0).start()
        if half:
            pltpu.make_async_copy(r_any, rows, sems.at[2]).start()
        fetch(1).start()

    for a in range(2):
        for b in range(8):
            lo = x_ref[b, a]
            hi = x_ref[b + 8, a]
            fold[128 * a:128 * a + 128, 128 * b:128 * b + 128] = lo + jnp.where(par == 0, hi, -hi)
    fetch(par).wait()
    res = lax.dot_general(
        t_ref[par].reshape(2 * PAIRS, NLON // 2), fold[...], (((1,), (1,)), ((), ())),
        preferred_element_type=F32,
    )
    if half:
        @pl.when(par == 0)
        def _():
            pltpu.make_async_copy(r_any, rows, sems.at[2]).wait()

    for ri in range(2):
        for a in range(2):
            rows[pl.ds(8 * par + 2 * (2 * half + a) + ri, PAIRS, stride=16), :] = (
                res[PAIRS * ri:PAIRS * ri + PAIRS, 128 * a:128 * a + 128]
            )

    if half:
        @pl.when(par == 1)
        def _():
            o_ref[...] = rows[...].reshape(o_ref.shape).astype(BF16)


def forward(x, table, rows=None):
    half = 0 if rows is None else 1
    anywhere = pl.BlockSpec(memory_space=pl.ANY)
    buffers = [
        pltpu.VMEM((256, NLON // 2), BF16),
        pltpu.VMEM((2, 2, PAIRS, NLON // 2), BF16),
        pltpu.SemaphoreType.DMA((3,)),
    ]
    if half == 0:
        operands = [in_vmem(x), table]
        out_specs = pl.BlockSpec((16 * PAIRS, 128), lambda g: (0, 0))
        out_shape = pltpu.HBM((16 * PAIRS, 128), F32)
    else:
        operands = [in_vmem(x), table, rows]
        out_specs = pl.BlockSpec((128, 48, 128), lambda g: (0, 0, 0))
        out_shape = pltpu.HBM((128, 48, 128), BF16)
        buffers.append(pltpu.VMEM((16 * PAIRS, 128), F32))
    return pl.pallas_call(
        functools.partial(forward_kernel, half),
        grid=(2,),
        in_specs=[IN_VMEM] + [anywhere] * (len(operands) - 1),
        out_specs=out_specs,
        out_shape=out_shape,
        scratch_shapes=buffers,
        compiler_params=vmem(56),
        name="forward",
    )(*operands)


CHUNK = 128


def legendre_kernel(a_ref, b_ref, m_ref, cos_ref, start_ref, w_ref, ana_ref, syn_ref, rows, state):
    chunk = pl.program_id(0)
    upper = lax.broadcasted_iota(jnp.int32, (8, 128), 0) < 4

    @pl.when(chunk == 0)
    def _():
        state[...] = jnp.zeros_like(state)

    cosine = [cos_ref[8 * v:8 * v + 8, :] for v in range(3)]
    orders = [m_ref[8 * v:8 * v + 8, :] for v in range(3)]

    def body(it, carry):
        prev, curr, logs, scale = carry
        for k in range(4):
            local = it * 4 + k
            degree = chunk * CHUNK + local
            nxt = []
            new_logs = []
            new_scale = []
            for v in range(3):
                at = degree * 6 + 2 * v
                a = jnp.where(upper, a_ref[at], a_ref[at + 1])
                b = jnp.where(upper, b_ref[at], b_ref[at + 1])
                first = orders[v] == degree
                start = start_ref[8 * v:8 * v + 8, :]
                val = jnp.where(first, 1.0, (a * cosine[v]) * curr[v] - b * prev[v])
                lg = jnp.where(first, start, logs[v])
                sc = jnp.where(first, start_ref[24 + 8 * v:32 + 8 * v, :], scale[v])
                row = pl.multiple_of(local * 24, 8) + 8 * v
                rows[pl.ds(row, 8), :] = val * sc
                nxt.append(val)
                new_logs.append(lg)
                new_scale.append(sc)
            prev, curr, logs, scale = curr, nxt, new_logs, new_scale
        grow = [jnp.maximum(1.0, jnp.maximum(jnp.abs(p), jnp.abs(c))) for p, c in zip(prev, curr)]
        inv = [1.0 / g for g in grow]
        prev = [p * i for p, i in zip(prev, inv)]
        curr = [c * i for c, i in zip(curr, inv)]
        logs = [l + jnp.log(g) for l, g in zip(logs, grow)]
        scale = [jnp.where(s > -1.0, jnp.where(o <= chunk * CHUNK + it * 4 + 3, jnp.exp(l), 0.0), 0.0)
                 for s, l, o in zip(scale, logs, orders)]
        return prev, curr, logs, scale

    init = tuple([state[24 * n + 8 * v:24 * n + 8 * v + 8, :] for v in range(3)] for n in range(4))
    final = lax.fori_loop(0, CHUNK // 4, body, init)
    for n in range(4):
        for v in range(3):
            state[24 * n + 8 * v:24 * n + 8 * v + 8, :] = final[n][v]
    for o in range(6):
        for jb in range(4):
            val = rows[pl.ds(4 * o + jb, CHUNK, stride=24), :]
            syn_ref[o, :, 128 * jb:128 * jb + 128] = val.astype(BF16)
            ana_ref[o, :, 128 * jb:128 * jb + 128] = (val * w_ref[jb:jb + 1, :]).astype(BF16)


def legendre_tables(orders):
    half = NLAT // 2
    colatitude = math.pi * (jnp.arange(half, dtype=F32) + 0.5) / NLAT
    sine = jnp.sin(colatitude)
    order_f = orders.astype(F32)
    log_start = (
        -0.5 * math.log(2.0)
        + 0.5 * (lax.lgamma(order_f + 1.5) - gamma_three_halves - lax.lgamma(order_f + 1.0))
    )[:, None] + order_f[:, None] * jnp.log(sine)[None, :]
    log_start = log_start.reshape(24, 128)
    start = jnp.concatenate((log_start, jnp.exp(log_start)))
    cosine = jnp.tile(jnp.cos(colatitude).reshape(4, 128), (6, 1))
    weight = (sine * (math.pi / NLAT)).reshape(4, 128)
    deg = jnp.arange(ORDERS, dtype=F32)[:, None]
    running = orders[None, :] < jnp.arange(ORDERS, dtype=jnp.int32)[:, None]
    denom_a = jnp.maximum(deg * deg - order_f * order_f, 1.0)
    coef_a = jnp.where(running, jnp.sqrt(jnp.maximum(4.0 * deg * deg - 1.0, 0.0) / denom_a), 0.0)
    numer_b = jnp.maximum((deg - 1.0) * (deg - 1.0) - order_f * order_f, 0.0)
    denom_b = jnp.maximum(4.0 * (deg - 1.0) * (deg - 1.0) - 1.0, 1.0)
    coef_b = coef_a * jnp.sqrt(numer_b / denom_b)
    order_rows = jnp.broadcast_to(jnp.repeat(orders, 4)[:, None], (24, 128))
    smem = pl.BlockSpec(memory_space=pltpu.SMEM)
    full = pl.BlockSpec((24, 128), lambda g: (0, 0))
    return pl.pallas_call(
        legendre_kernel,
        grid=(ORDERS // CHUNK,),
        in_specs=[
            smem, smem, full, full,
            pl.BlockSpec((48, 128), lambda g: (0, 0)),
            pl.BlockSpec((4, 128), lambda g: (0, 0)),
        ],
        out_specs=[pl.BlockSpec((6, CHUNK, half), lambda g: (0, g, 0))] * 2,
        out_shape=[pltpu.HBM((6, ORDERS, half), BF16)] * 2,
        scratch_shapes=[pltpu.VMEM((CHUNK * 24, 128), F32), pltpu.VMEM((96, 128), F32)],
        name="legendre_tables",
    )(coef_a.reshape(-1), coef_b.reshape(-1), order_rows, cosine, start, weight)


def filter_kernel(slot_ref, ord_ref, f_ref, ana_ref, syn_ref, spec_ref, back_ref):
    sub = lax.broadcasted_iota(jnp.int32, (128, 128), 0)
    flip = jnp.where(sub + lane_ids((128, 128)) == 127, 1.0, 0.0).astype(BF16)
    pair = pl.program_id(0)
    above = (ord_ref[2 * pair] < ORDERS // 2).astype(jnp.int32)
    for k, low in ((above, ORDERS // 2), (1 - above, 0)):
        width = ORDERS - low
        o = 2 * pair + k
        order = ord_ref[o]
        plus = []
        minus = []
        for c in range(4):
            north = f_ref[c, :, o].astype(F32).reshape(128, 128)
            south = f_ref[7 - c, :, o].astype(F32).reshape(128, 128).astype(BF16)
            south = jnp.dot(south, flip, preferred_element_type=F32)
            plus.append((north + south).astype(BF16))
            minus.append((north - south).astype(BF16))
        both = jnp.concatenate(
            [jnp.concatenate(plus, axis=1), jnp.concatenate(minus, axis=1)], axis=0
        )
        coef = lax.dot_general(
            both, ana_ref[k, low:, :], (((1,), (1,)), ((), ())), preferred_element_type=F32
        )
        even = ((lane_ids((128, width)) - order) & 1) == 0
        spec = jnp.where(even, coef[:128], coef[128:])
        if low:
            spec_ref[slot_ref[o] & 1, :, :low] = jnp.zeros((128, low), F32)
        spec_ref[slot_ref[o] & 1, :, low:] = spec
        parts = jnp.concatenate([jnp.where(even, spec, 0.0), jnp.where(even, 0.0, spec)], axis=0)
        grid = jnp.dot(parts.astype(BF16), syn_ref[k, low:, :], preferred_element_type=F32)
        factor = jnp.where(order == 0, 0.5, 1.0)
        north = (grid[:128] + grid[128:]) * factor
        south = ((grid[:128] - grid[128:]) * factor).astype(BF16)
        for c in range(4):
            cut = slice(128 * c, 128 * c + 128)
            back_ref[c, :, k] = north[:, cut].reshape(16, 8, 128).astype(BF16)
            turned = jnp.dot(south[:, cut], flip, preferred_element_type=F32)
            back_ref[7 - c, :, k] = turned.reshape(16, 8, 128).astype(BF16)


def legendre_filter(fourier, analysis, synthesis, orders, slots):
    table = pl.BlockSpec((2, ORDERS, NLAT // 2), lambda p, *_: (p, 0, 0))
    blocks = pl.BlockSpec((8, 16, 2, 8, 128), lambda p, *_: (0, 0, p, 0, 0))
    return pl.pallas_call(
        filter_kernel,
        grid_spec=pltpu.PrefetchScalarGridSpec(
            num_scalar_prefetch=2,
            grid=(3,),
            in_specs=[IN_VMEM, table, table],
            out_specs=[
                pl.BlockSpec((2, 128, ORDERS), lambda p, *_: (p, 0, 0)),
                blocks,
            ],
        ),
        out_shape=[
            pltpu.HBM((6, 128, ORDERS), F32),
            pltpu.HBM((8, 16, 6, 8, 128), BF16),
        ],
        compiler_params=vmem(56),
        name="legendre_filter",
    )(slots, orders, in_vmem(fourier), analysis, synthesis)


def inverse_kernel(y_ref, t_any, o_ref, rows, cols, t_ref, sems):
    step = pl.program_id(0)
    width = NLON // 2 // 2

    def fetch(n, par):
        at = pl.ds(pl.multiple_of(n * width, width), width)
        return pltpu.make_async_copy(
            t_any.at[par, :, :, at], t_ref.at[n, par], sems.at[n, par]
        )

    @pl.when(step == 0)
    def _():
        for n in range(2):
            for par in range(2):
                fetch(n, par).start()
        rows[...] = y_ref[...].astype(F32).reshape(rows.shape)
        for par in range(2):
            for ri in range(2):
                for a in range(4):
                    cols[par, PAIRS * ri:PAIRS * ri + PAIRS, 128 * a:128 * a + 128] = (
                        rows[pl.ds(8 * par + 2 * a + ri, PAIRS, stride=16), :].astype(BF16)
                    )

    sums = []
    for par in range(2):
        fetch(step, par).wait()
        res = lax.dot_general(
            cols[par], t_ref[step, par].reshape(2 * PAIRS, width), (((0,), (0,)), ((), ())),
            preferred_element_type=F32,
        )
        sums.append(res * (2.0 / NLON))
    low = (sums[0] + sums[1]).astype(BF16)
    high = (sums[0] - sums[1]).astype(BF16)
    for b in range(width // 128):
        o_ref[0, b] = low[:, 128 * b:128 * b + 128].reshape(4, 128, 128)
        o_ref[1, b] = high[:, 128 * b:128 * b + 128].reshape(4, 128, 128)


def inverse(y, table):
    steps = 2
    width = NLON // 2 // steps
    out = pl.pallas_call(
        inverse_kernel,
        grid=(steps,),
        in_specs=[
            IN_VMEM,
            pl.BlockSpec(memory_space=pl.ANY),
        ],
        out_specs=pl.BlockSpec((2, width // 128, 4, 128, 128), lambda g: (0, g, 0, 0, 0)),
        out_shape=pltpu.HBM((2, 8, 4, 128, 128), BF16),
        scratch_shapes=[
            pltpu.VMEM((128 * 48, 128), F32),
            pltpu.VMEM((2, 2 * PAIRS, 512), BF16),
            pltpu.VMEM((steps, 2, 2, PAIRS, width), BF16),
            pltpu.SemaphoreType.DMA((steps, 2)),
        ],
        compiler_params=vmem(56),
        name="inverse",
    )(in_vmem(y), table)
    return out.reshape(16, 4, 128, 128)


def update_kernel(se_ref, sp_ref, f_ref, old_ent, old_pres, oe_ref, op_ref):
    at = pl.ds(8 * pl.program_id(0), 8)
    oe_ref[...] = se_ref[...] + 0.5 * f_ref[0, at].astype(F32)
    op_ref[...] = sp_ref[...] + 0.5 * f_ref[1, at].astype(F32)


def update(start_entropy, start_pressure, filtered, ent, pres):
    whole = pl.BlockSpec((8, ROWS, COLS), lambda g: (g, 0, 0))
    anywhere = pl.BlockSpec(memory_space=pl.ANY)
    return pl.pallas_call(
        update_kernel,
        grid=(FLEV // 8,),
        in_specs=[whole, whole, IN_VMEM, anywhere, anywhere],
        out_specs=[whole, whole],
        out_shape=[pltpu.HBM((LEV, ROWS, COLS), F32)] * 2,
        input_output_aliases={3: 0, 4: 1},
        compiler_params=vmem(56),
        name="update",
    )(start_entropy, start_pressure, in_vmem(filtered), ent, pres)


def per_device(entropy, zonal_flux, meridional_flux, start_entropy, start_pressure, order_slot):
    n_lat = lax.axis_size("lat")
    n_lon = lax.axis_size("lonr")
    pairs = order_slot.reshape(PAIRS, 2)
    first_even = (pairs[:, 0] % 2) == 0
    even = jnp.where(first_even, pairs[:, 0], pairs[:, 1])
    odd = jnp.where(first_even, pairs[:, 1], pairs[:, 0])
    block = lax.axis_index("lat") * n_lon + lax.axis_index("lonr")
    both = jnp.stack((even, odd), axis=1)
    orders = lax.dynamic_slice_in_dim(both, block * 3, 3).reshape(6)
    swap = jnp.where(first_even, 0, 1).astype(jnp.int32)
    swap = lax.dynamic_slice_in_dim(swap, block * 3, 3)
    base = 2 * jnp.arange(3, dtype=jnp.int32)
    slots = jnp.stack((base + swap, base + 1 - swap), axis=1).reshape(6)

    first = (lax.axis_index("lat") * ROWS).astype(jnp.int32).reshape(1)
    side, south, north, fs, rc = edges(first, entropy, zonal_flux, meridional_flux)
    ring = range(n_lon)
    from_west = lax.ppermute(side, "lonr", [(i, (i + 1) % n_lon) for i in ring])
    from_east = lax.ppermute(side, "lonr", [((i + 1) % n_lon, i) for i in ring])
    from_north = lax.ppermute(south, "lat", [(i, i + 1) for i in range(n_lat - 1)])
    from_south = lax.ppermute(north, "lat", [(i + 1, i) for i in range(n_lat - 1)])
    table = fourier_table(jnp.stack((even, odd)))
    fields = (entropy, zonal_flux, meridional_flux)
    halos = (from_west, from_east, side, from_north, from_south)

    def exchange(items):
        return lax.all_to_all(
            items.reshape(16, 2, ROWS, COLS), "lonr", split_axis=0, concat_axis=0, tiled=True
        )

    first_items = exchange(tendencies(fields, halos, (fs, rc), half=0))
    second_items = exchange(tendencies(fields, halos, (fs, rc), half=1))
    ent, pres = tendencies(fields, halos, (fs, rc), starts=[start_entropy, start_pressure])
    rows = forward(first_items, table)
    spectral = forward(second_items, table, rows)
    analysis, synthesis = legendre_tables(orders)
    spectral = lax.all_to_all(
        spectral, ("lat", "lonr"), split_axis=0, concat_axis=0, tiled=True
    )
    spectrum, back = legendre_filter(
        spectral.reshape(8, 16, 6, 8, 128), analysis, synthesis, orders, slots
    )
    back = lax.all_to_all(
        back.reshape(128, 48, 128), ("lat", "lonr"), split_axis=0, concat_axis=0, tiled=True
    )
    filtered = inverse(back, table)
    filtered = lax.all_to_all(filtered, "lonr", split_axis=0, concat_axis=0, tiled=True)
    new_entropy, new_pressure = update(
        start_entropy, start_pressure, filtered.reshape(2, FLEV, ROWS, COLS), ent, pres
    )
    return new_entropy, new_pressure, spectrum.reshape(6, 64, 2, ORDERS)


def solution(mesh):
    cube = P(None, "lat", "lonr")
    return jax.shard_map(
        per_device,
        mesh=mesh,
        in_specs=(cube, cube, cube, cube, cube, P()),
        out_specs=(cube, cube, P(("lat", "lonr"), None, None, None)),
        check_vma=False,
    )
```

```python
import functools
import math

import jax
import jax.numpy as jnp
from jax import lax
from jax.experimental import pallas as pl
from jax.experimental.pallas import tpu as pltpu
import numpy as np
from jax.sharding import PartitionSpec as P

FLEV = 32
LEV = 40
NLAT = 1024
NLON = 2048
ORDERS = 768
PAIRS = ORDERS // 2
ROWS = 128
COLS = 128
F32 = jnp.float32
BF16 = jnp.bfloat16

gamma_three_halves = 0.5 * math.log(math.pi) - math.log(2.0)


def vmem(mib):
    return pltpu.CompilerParams(vmem_limit_bytes=mib << 20)


IN_VMEM = pl.BlockSpec(memory_space=pltpu.VMEM)


def in_vmem(x):
    return pltpu.with_memory_space_constraint(x, pltpu.VMEM)


def lane_ids(shape):
    return lax.broadcasted_iota(jnp.int32, shape, len(shape) - 1)


def sine_of(n):
    x = jnp.minimum(n, NLAT - n) * (math.pi / NLAT)
    square = x * x
    total = jnp.full_like(x, 1.0 / math.factorial(13))
    for power in (11, 9, 7, 5, 3, 1):
        total = total * square + (-1.0) ** (power // 2) / math.factorial(power)
    return total * x


def edges_kernel(
    first_ref, s_any, u_any, v_ref, side_ref, south_ref, north_ref, fs_ref, rc_ref,
    s_ref, u_ref, sems
):
    lane = lane_ids((8, 128))
    owner = ((lane + 3) & 127) >> 3
    part = lane & 7
    parts = LEV // 8

    def fetch(n, g):
        at = pl.ds(8 * g, 8)
        src = (s_any, u_any)[n]
        dst = (s_ref, u_ref)[n]
        return pltpu.make_async_copy(src.at[at], dst.at[at], sems.at[n, g])

    for g in range(parts):
        for n in range(2):
            fetch(n, g).start()
    at = first_ref[0] - 8 + lax.broadcasted_iota(jnp.int32, (136, 128), 0)
    sines = sine_of((at + 1).astype(F32))
    fs_ref[...] = jnp.where((at >= 0) & (at < NLAT - 1), sines, 0.0)
    rc_ref[...] = 1.0 / sine_of(at[8:].astype(F32) + 0.5)

    def four_levels(q, carry):
        for k in range(4):
            lev = 4 * q + k
            side = jnp.zeros((8, 128), F32)
            flux = jnp.zeros((8, 128), F32)
            for i in range(16):
                s = s_ref[lev, pl.ds(8 * i, 8), :]
                u = u_ref[lev, pl.ds(8 * i, 8), :]
                side = jnp.where(owner == i, pltpu.roll(s, 8 * i, 1) if i else s, side)
                flux = jnp.where(owner == i, pltpu.roll(u, 8 * i, 1) if i else u, flux)
            side_ref[lev] = jnp.where(part == 4, pltpu.roll(flux, 125, 1), side)
            south_ref[lev, 0:3, :] = s_ref[lev, 125:128, :]
            north_ref[lev] = s_ref[lev, 0:4, :]
        return carry

    for g in range(parts):
        for n in range(2):
            fetch(n, g).wait()
        lax.fori_loop(2 * g, 2 * g + 2, four_levels, 0)
    for lev in range(LEV):
        south_ref[lev, 3:4, :] = v_ref[lev, 7:8, :]


def edges(first, entropy, zonal, merid):
    anywhere = pl.BlockSpec(memory_space=pl.ANY)
    return pl.pallas_call(
        edges_kernel,
        grid=(1,),
        in_specs=[pl.BlockSpec(memory_space=pltpu.SMEM), anywhere, anywhere, pl.BlockSpec((LEV, 8, COLS), lambda g: (0, ROWS // 8 - 1, 0))],
        out_specs=[pl.BlockSpec((LEV, n, 128), lambda g: (0, 0, 0)) for n in (8, 4, 4)]
        + [pl.BlockSpec((n, 128), lambda g: (0, 0)) for n in (136, 128)],
        out_shape=[
            pltpu.HBM((LEV, 8, 128), F32),
            pltpu.HBM((LEV, 4, 128), F32),
            pltpu.HBM((LEV, 4, 128), F32),
            pltpu.HBM((136, 128), F32),
            pltpu.HBM((128, 128), F32),
        ],
        scratch_shapes=[pltpu.VMEM((LEV, ROWS, COLS), F32)] * 2
        + [pltpu.SemaphoreType.DMA((2, LEV // 8))],
        name="edges",
    )(first, entropy, zonal, merid)


def stencil(x0, x1, x2, x3, x4, x5):
    return (37.0 * (x2 + x3) - 8.0 * (x1 + x4) + (x0 + x5)) * (1.0 / 60.0)


def stencil_matrices():
    weights = {-2: 1.0, -1: -8.0, 0: 37.0, 1: 37.0, 2: -8.0, 3: 1.0}
    along = np.zeros((256, 256), np.float32)
    across = np.zeros((128, 136), np.float32)
    for face in range(128):
        for shift, weight in weights.items():
            cell = face + shift
            along[cell if 0 <= cell < 128 else 128 + cell % 128 if cell >= 128 else 256 + cell, face] = weight
            across[face, cell if 0 <= cell < 128 else 128 + 4 + cell % 128 if cell >= 128 else 128 + 3 + cell] = weight
    along[128 + 3, 128 + 127] = 1.0
    along[128 + 124, 128] = 1.0
    return along, across


def split(x):
    high = x.astype(BF16)
    return high, (x - high.astype(F32)).astype(BF16)


def tend_kernel(*refs):
    (s_ref, u_ref, v_ref, hw_ref, he_ref, ow_ref, hn_ref, hs_ref, fs_ref, rc_ref, along_ref,
     across_ref) = refs[:12]
    cells, face, mext = refs[-3:]
    wide = s_ref.shape[1]
    lane = lane_ids((ROWS, COLS))
    small = lane_ids((8, 128)) & 7
    across = across_ref[...]

    def prepare(lev):
        west = hw_ref[lev // wide, lev % wide]
        own = ow_ref[lev // wide, lev % wide]
        edge = stencil(
            pltpu.roll(west, 6, 1), pltpu.roll(west, 5, 1), pltpu.roll(west, 4, 1),
            pltpu.roll(own, 3, 1), pltpu.roll(own, 2, 1), pltpu.roll(own, 1, 1),
        )
        edge = edge * pltpu.roll(west, 7, 1)
        rim = jnp.where(small < 3, he_ref[lev // wide, lev % wide], jnp.where(small == 3, edge, west))
        rim = jnp.concatenate([pltpu.roll(rim, (128 - 8 * i) % 128, 1) for i in range(16)])
        s = s_ref[lev // wide, lev % wide]
        s_hi, s_lo = split(s)
        r_hi, r_lo = split(rim)
        at = slice(128 * lev, 128 * lev + 128)
        cells[at, 0:128] = s_hi
        cells[at, 128:256] = r_hi
        cells[at, 256:384] = s_lo
        cells[at, 384:512] = r_lo
        h_hi, h_lo = split(jnp.concatenate([hn_ref[lev // wide, lev % wide], hs_ref[lev // wide, lev % wide]]))
        face[lev, :, 256:384] = jnp.dot(
            across, jnp.concatenate([s_hi, s_lo, h_hi, h_lo]), preferred_element_type=F32
        )

    def multiply(part):
        rows = slice(512 * part, 512 * part + 512)
        res = jnp.dot(cells[rows, :], along_ref[...], preferred_element_type=F32)
        face[4 * part:4 * part + 4, :, 0:256] = res.reshape(4, 128, 256)

    def level(lev):
        half = lev % 4
        u = u_ref[lev // wide, lev % wide]
        z = (u * (1.0 / 60.0)) * face[lev, :, 0:128]
        rim = face[lev, :, 128:256]
        dz = z - pltpu.roll(jnp.where(lane == COLS - 1, rim, z), 1, 1)
        du = u - jnp.where(lane == 0, rim, pltpu.roll(u, 1, 1))
        fv = v_ref[lev // wide, lev % wide] * fs_ref[8:136, :]
        fv_top = hn_ref[lev // wide, lev % wide, 3:4, :] * fs_ref[7:8, :]
        top = [hn_ref[lev // wide, lev % wide, o:o + 1, :] for o in range(3)] + [s_ref[lev // wide, lev % wide, o:o + 1, :] for o in range(3)]
        m = fv * (face[lev, :, 256:384] * (1.0 / 60.0))
        mext[half, 0, 7:8, :] = fv_top * stencil(*top)
        mext[half, 0, 8:136, :] = m
        mext[half, 1, 7:8, :] = fv_top
        mext[half, 1, 8:136, :] = fv
        rc = rc_ref[...]
        ent = -(dz + (m - mext[half, 0, 7:135, :]) * rc)
        pres = -0.3 * (du + (fv - mext[half, 1, 7:135, :]) * rc)
        return ent, pres

    def put(lev, ent, pres):
        if len(refs) == 16:
            item_ref = refs[12]
            item_ref[0, lev // 2, lev % 2] = ent.astype(BF16)
            item_ref[1, lev // 2, lev % 2] = pres.astype(BF16)
        else:
            se_ref, sp_ref, ent_ref, pres_ref = refs[12:16]
            ent_ref[lev] = se_ref[lev] + 0.5 * ent
            pres_ref[lev] = sp_ref[lev] + 0.5 * pres

    for lev in range(4):
        prepare(lev)
    multiply(0)
    for lev in range(4, 8):
        prepare(lev)
    multiply(1)
    for lev in range(8):
        put(lev, *level(lev))


def tendencies(fields, halos, factors, starts=None, half=None):
    groups = LEV // 4
    if half is None:
        deep, wide, steps = 2, 4, 1

        def at(g):
            return (FLEV // 8, 0)
    else:
        deep, wide, steps = 4, 2, 2

        def at(g):
            return (g, half)

    def spec(rows):
        return pl.BlockSpec((deep, wide, rows, 128), lambda g: at(g) + (0, 0))

    along, across = stencil_matrices()
    along = jnp.asarray(np.concatenate((along, along)), BF16)
    across = np.concatenate(
        (across[:, :128], across[:, :128], across[:, 128:], across[:, 128:]), axis=1
    )
    operands = [x.reshape(groups, 4, *x.shape[1:]) for x in (*fields, *halos)]
    in_specs = [spec(x.shape[2]) for x in operands]
    operands += [*factors, along, jnp.asarray(across, BF16)]
    in_specs += [
        pl.BlockSpec((136, 128), lambda g: (0, 0)),
        pl.BlockSpec((128, 128), lambda g: (0, 0)),
        pl.BlockSpec((512, 256), lambda g: (0, 0)),
        pl.BlockSpec((128, 272), lambda g: (0, 0)),
    ]
    if half is None:
        tail = pl.BlockSpec((8, ROWS, COLS), lambda g: (FLEV // 8, 0, 0))
        operands += starts
        in_specs += [tail, tail]
        out_specs = [tail, tail]
        out_shape = [pltpu.HBM((LEV, ROWS, COLS), F32)] * 2
    else:
        out_specs = pl.BlockSpec((2, 4, 2, ROWS, COLS), lambda g: (0, g, 0, 0, 0))
        out_shape = pltpu.HBM((2, 8, 2, ROWS, COLS), BF16)
    return pl.pallas_call(
        tend_kernel,
        grid=(steps,),
        in_specs=in_specs,
        out_specs=out_specs,
        out_shape=out_shape,
        scratch_shapes=[
            pltpu.VMEM((1024, 512), BF16),
            pltpu.VMEM((8, 128, 384), F32),
            pltpu.VMEM((4, 2, 136, 128), F32),
        ],
        name="tendencies" if half is not None else "tail",
    )(*operands)


def table_kernel(base_ref, turn_ref, out_ref):
    for par in range(2):
        c = base_ref[par, 0]
        s = base_ref[par, 1]
        for b in range(8):
            tc = jnp.broadcast_to(turn_ref[par, :, b:b + 1], c.shape)
            ts = jnp.broadcast_to(turn_ref[par, :, 8 + b:9 + b], c.shape)
            out_ref[par, 0, :, 128 * b:128 * b + 128] = (c * tc - s * ts).astype(BF16)
            out_ref[par, 1, :, 128 * b:128 * b + 128] = (s * tc + c * ts).astype(BF16)


def fourier_table(even_odd):
    def angles(steps):
        product = (even_odd[:, :, None] * steps[None, None, :]) % NLON
        return (2.0 * math.pi / NLON) * product.astype(F32)

    near = angles(jnp.arange(128, dtype=jnp.int32))
    far = angles(128 * jnp.arange(8, dtype=jnp.int32))
    base = jnp.stack((jnp.cos(near), jnp.sin(near)), axis=1)
    turn = jnp.concatenate((jnp.cos(far), jnp.sin(far)), axis=2)
    tile = 96
    return pl.pallas_call(
        table_kernel,
        grid=(PAIRS // tile,),
        in_specs=[
            pl.BlockSpec((2, 2, tile, 128), lambda g: (0, 0, g, 0)),
            pl.BlockSpec((2, tile, 16), lambda g: (0, g, 0)),
        ],
        out_specs=pl.BlockSpec((2, 2, tile, NLON // 2), lambda g: (0, 0, g, 0)),
        out_shape=pltpu.HBM((2, 2, PAIRS, NLON // 2), BF16),
        name="longitude_table",
    )(base, turn)


def forward_kernel(half, *refs):
    if half == 0:
        x_ref, t_any, rows, fold, t_ref, sems = refs
    else:
        x_ref, t_any, r_any, o_ref, fold, t_ref, sems, rows = refs
    par = pl.program_id(0)

    def fetch(n):
        return pltpu.make_async_copy(t_any.at[n], t_ref.at[n], sems.at[n])

    @pl.when(par == 0)
    def _():
        fetch(0).start()
        if half:
            pltpu.make_async_copy(r_any, rows, sems.at[2]).start()
        fetch(1).start()

    for a in range(2):
        for b in range(8):
            lo = x_ref[b, a]
            hi = x_ref[b + 8, a]
            fold[128 * a:128 * a + 128, 128 * b:128 * b + 128] = lo + jnp.where(par == 0, hi, -hi)
    fetch(par).wait()
    res = lax.dot_general(
        t_ref[par].reshape(2 * PAIRS, NLON // 2), fold[...], (((1,), (1,)), ((), ())),
        preferred_element_type=F32,
    )
    if half:
        @pl.when(par == 0)
        def _():
            pltpu.make_async_copy(r_any, rows, sems.at[2]).wait()

    for ri in range(2):
        for a in range(2):
            rows[pl.ds(8 * par + 2 * (2 * half + a) + ri, PAIRS, stride=16), :] = (
                res[PAIRS * ri:PAIRS * ri + PAIRS, 128 * a:128 * a + 128]
            )

    if half:
        @pl.when(par == 1)
        def _():
            o_ref[...] = rows[...].reshape(o_ref.shape).astype(BF16)


def forward(x, table, rows=None):
    half = 0 if rows is None else 1
    anywhere = pl.BlockSpec(memory_space=pl.ANY)
    buffers = [
        pltpu.VMEM((256, NLON // 2), BF16),
        pltpu.VMEM((2, 2, PAIRS, NLON // 2), BF16),
        pltpu.SemaphoreType.DMA((3,)),
    ]
    if half == 0:
        operands = [in_vmem(x), table]
        out_specs = pl.BlockSpec((16 * PAIRS, 128), lambda g: (0, 0))
        out_shape = pltpu.HBM((16 * PAIRS, 128), F32)
    else:
        operands = [in_vmem(x), table, rows]
        out_specs = pl.BlockSpec((128, 48, 128), lambda g: (0, 0, 0))
        out_shape = pltpu.HBM((128, 48, 128), BF16)
        buffers.append(pltpu.VMEM((16 * PAIRS, 128), F32))
    return pl.pallas_call(
        functools.partial(forward_kernel, half),
        grid=(2,),
        in_specs=[IN_VMEM] + [anywhere] * (len(operands) - 1),
        out_specs=out_specs,
        out_shape=out_shape,
        scratch_shapes=buffers,
        compiler_params=vmem(56),
        name="forward",
    )(*operands)


CHUNK = 128


def legendre_kernel(a_ref, b_ref, m_ref, cos_ref, start_ref, w_ref, ana_ref, syn_ref, rows, state):
    chunk = pl.program_id(0)
    upper = lax.broadcasted_iota(jnp.int32, (8, 128), 0) < 4

    @pl.when(chunk == 0)
    def _():
        state[...] = jnp.zeros_like(state)

    cosine = [cos_ref[8 * v:8 * v + 8, :] for v in range(3)]
    orders = [m_ref[8 * v:8 * v + 8, :] for v in range(3)]

    def body(it, carry):
        prev, curr, logs, scale = carry
        for k in range(4):
            local = it * 4 + k
            degree = chunk * CHUNK + local
            nxt = []
            new_logs = []
            new_scale = []
            for v in range(3):
                at = degree * 6 + 2 * v
                a = jnp.where(upper, a_ref[at], a_ref[at + 1])
                b = jnp.where(upper, b_ref[at], b_ref[at + 1])
                first = orders[v] == degree
                start = start_ref[8 * v:8 * v + 8, :]
                val = jnp.where(first, 1.0, (a * cosine[v]) * curr[v] - b * prev[v])
                lg = jnp.where(first, start, logs[v])
                sc = jnp.where(first, start_ref[24 + 8 * v:32 + 8 * v, :], scale[v])
                row = pl.multiple_of(local * 24, 8) + 8 * v
                rows[pl.ds(row, 8), :] = val * sc
                nxt.append(val)
                new_logs.append(lg)
                new_scale.append(sc)
            prev, curr, logs, scale = curr, nxt, new_logs, new_scale
        grow = [jnp.maximum(1.0, jnp.maximum(jnp.abs(p), jnp.abs(c))) for p, c in zip(prev, curr)]
        inv = [1.0 / g for g in grow]
        prev = [p * i for p, i in zip(prev, inv)]
        curr = [c * i for c, i in zip(curr, inv)]
        logs = [l + jnp.log(g) for l, g in zip(logs, grow)]
        scale = [jnp.where(s > -1.0, jnp.where(o <= chunk * CHUNK + it * 4 + 3, jnp.exp(l), 0.0), 0.0)
                 for s, l, o in zip(scale, logs, orders)]
        return prev, curr, logs, scale

    init = tuple([state[24 * n + 8 * v:24 * n + 8 * v + 8, :] for v in range(3)] for n in range(4))
    final = lax.fori_loop(0, CHUNK // 4, body, init)
    for n in range(4):
        for v in range(3):
            state[24 * n + 8 * v:24 * n + 8 * v + 8, :] = final[n][v]
    for o in range(6):
        for jb in range(4):
            val = rows[pl.ds(4 * o + jb, CHUNK, stride=24), :]
            syn_ref[o, :, 128 * jb:128 * jb + 128] = val.astype(BF16)
            ana_ref[o, :, 128 * jb:128 * jb + 128] = (val * w_ref[jb:jb + 1, :]).astype(BF16)


def legendre_inputs(orders):
    half = NLAT // 2
    colatitude = math.pi * (jnp.arange(half, dtype=F32) + 0.5) / NLAT
    sine = jnp.sin(colatitude)
    order_f = orders.astype(F32)
    log_start = (
        -0.5 * math.log(2.0)
        + 0.5 * (lax.lgamma(order_f + 1.5) - gamma_three_halves - lax.lgamma(order_f + 1.0))
    )[:, None] + order_f[:, None] * jnp.log(sine)[None, :]
    log_start = log_start.reshape(24, 128)
    start = jnp.concatenate((log_start, jnp.exp(log_start)))
    cosine = jnp.tile(jnp.cos(colatitude).reshape(4, 128), (6, 1))
    weight = (sine * (math.pi / NLAT)).reshape(4, 128)
    deg = jnp.arange(ORDERS, dtype=F32)[:, None]
    running = orders[None, :] < jnp.arange(ORDERS, dtype=jnp.int32)[:, None]
    denom_a = jnp.maximum(deg * deg - order_f * order_f, 1.0)
    coef_a = jnp.where(running, jnp.sqrt(jnp.maximum(4.0 * deg * deg - 1.0, 0.0) / denom_a), 0.0)
    numer_b = jnp.maximum((deg - 1.0) * (deg - 1.0) - order_f * order_f, 0.0)
    denom_b = jnp.maximum(4.0 * (deg - 1.0) * (deg - 1.0) - 1.0, 1.0)
    coef_b = coef_a * jnp.sqrt(numer_b / denom_b)
    order_rows = jnp.broadcast_to(jnp.repeat(orders, 4)[:, None], (24, 128))
    return [coef_a.reshape(-1), coef_b.reshape(-1), order_rows, cosine, start, weight]


def legendre_tables(inputs):
    half = NLAT // 2
    smem = pl.BlockSpec(memory_space=pltpu.SMEM)
    full = pl.BlockSpec((24, 128), lambda g: (0, 0))
    return pl.pallas_call(
        legendre_kernel,
        grid=(ORDERS // CHUNK,),
        in_specs=[
            smem, smem, full, full,
            pl.BlockSpec((48, 128), lambda g: (0, 0)),
            pl.BlockSpec((4, 128), lambda g: (0, 0)),
        ],
        out_specs=[pl.BlockSpec((6, CHUNK, half), lambda g: (0, g, 0))] * 2,
        out_shape=[pltpu.HBM((6, ORDERS, half), BF16)] * 2,
        scratch_shapes=[pltpu.VMEM((CHUNK * 24, 128), F32), pltpu.VMEM((96, 128), F32)],
        name="legendre_tables",
    )(*inputs)


def filter_kernel(slot_ref, ord_ref, f_ref, ana_ref, syn_ref, spec_ref, back_ref):
    sub = lax.broadcasted_iota(jnp.int32, (128, 128), 0)
    flip = jnp.where(sub + lane_ids((128, 128)) == 127, 1.0, 0.0).astype(BF16)
    pair = pl.program_id(0)
    above = (ord_ref[2 * pair] < ORDERS // 2).astype(jnp.int32)
    for k, low in ((above, ORDERS // 2), (1 - above, 0)):
        width = ORDERS - low
        o = 2 * pair + k
        order = ord_ref[o]
        plus = []
        minus = []
        for c in range(4):
            north = f_ref[c, :, o].astype(F32).reshape(128, 128)
            south = f_ref[7 - c, :, o].astype(F32).reshape(128, 128).astype(BF16)
            south = jnp.dot(south, flip, preferred_element_type=F32)
            plus.append((north + south).astype(BF16))
            minus.append((north - south).astype(BF16))
        both = jnp.concatenate(
            [jnp.concatenate(plus, axis=1), jnp.concatenate(minus, axis=1)], axis=0
        )
        coef = lax.dot_general(
            both, ana_ref[k, low:, :], (((1,), (1,)), ((), ())), preferred_element_type=F32
        )
        even = ((lane_ids((128, width)) - order) & 1) == 0
        spec = jnp.where(even, coef[:128], coef[128:])
        if low:
            spec_ref[slot_ref[o] & 1, :, :low] = jnp.zeros((128, low), F32)
        spec_ref[slot_ref[o] & 1, :, low:] = spec
        parts = jnp.concatenate([jnp.where(even, spec, 0.0), jnp.where(even, 0.0, spec)], axis=0)
        grid = jnp.dot(parts.astype(BF16), syn_ref[k, low:, :], preferred_element_type=F32)
        factor = jnp.where(order == 0, 0.5, 1.0)
        north = (grid[:128] + grid[128:]) * factor
        south = ((grid[:128] - grid[128:]) * factor).astype(BF16)
        for c in range(4):
            cut = slice(128 * c, 128 * c + 128)
            back_ref[c, :, k] = north[:, cut].reshape(16, 8, 128).astype(BF16)
            turned = jnp.dot(south[:, cut], flip, preferred_element_type=F32)
            back_ref[7 - c, :, k] = turned.reshape(16, 8, 128).astype(BF16)


def legendre_filter(fourier, analysis, synthesis, orders, slots):
    table = pl.BlockSpec((2, ORDERS, NLAT // 2), lambda p, *_: (p, 0, 0))
    blocks = pl.BlockSpec((8, 16, 2, 8, 128), lambda p, *_: (0, 0, p, 0, 0))
    return pl.pallas_call(
        filter_kernel,
        grid_spec=pltpu.PrefetchScalarGridSpec(
            num_scalar_prefetch=2,
            grid=(3,),
            in_specs=[IN_VMEM, table, table],
            out_specs=[
                pl.BlockSpec((2, 128, ORDERS), lambda p, *_: (p, 0, 0)),
                blocks,
            ],
        ),
        out_shape=[
            pltpu.HBM((6, 128, ORDERS), F32),
            pltpu.HBM((8, 16, 6, 8, 128), BF16),
        ],
        compiler_params=vmem(56),
        name="legendre_filter",
    )(slots, orders, in_vmem(fourier), analysis, synthesis)


def inverse_kernel(y_ref, t_any, o_ref, rows, cols, t_ref, sems):
    step = pl.program_id(0)
    width = NLON // 2 // 2

    def fetch(n, par):
        at = pl.ds(pl.multiple_of(n * width, width), width)
        return pltpu.make_async_copy(
            t_any.at[par, :, :, at], t_ref.at[n, par], sems.at[n, par]
        )

    @pl.when(step == 0)
    def _():
        for n in range(2):
            for par in range(2):
                fetch(n, par).start()
        rows[...] = y_ref[...].astype(F32).reshape(rows.shape)
        for par in range(2):
            for ri in range(2):
                for a in range(4):
                    cols[par, PAIRS * ri:PAIRS * ri + PAIRS, 128 * a:128 * a + 128] = (
                        rows[pl.ds(8 * par + 2 * a + ri, PAIRS, stride=16), :].astype(BF16)
                    )

    sums = []
    for par in range(2):
        fetch(step, par).wait()
        res = lax.dot_general(
            cols[par], t_ref[step, par].reshape(2 * PAIRS, width), (((0,), (0,)), ((), ())),
            preferred_element_type=F32,
        )
        sums.append(res * (2.0 / NLON))
    low = (sums[0] + sums[1]).astype(BF16)
    high = (sums[0] - sums[1]).astype(BF16)
    for b in range(width // 128):
        o_ref[0, b] = low[:, 128 * b:128 * b + 128].reshape(4, 128, 128)
        o_ref[1, b] = high[:, 128 * b:128 * b + 128].reshape(4, 128, 128)


def inverse(y, table):
    steps = 2
    width = NLON // 2 // steps
    out = pl.pallas_call(
        inverse_kernel,
        grid=(steps,),
        in_specs=[
            IN_VMEM,
            pl.BlockSpec(memory_space=pl.ANY),
        ],
        out_specs=pl.BlockSpec((2, width // 128, 4, 128, 128), lambda g: (0, g, 0, 0, 0)),
        out_shape=pltpu.HBM((2, 8, 4, 128, 128), BF16),
        scratch_shapes=[
            pltpu.VMEM((128 * 48, 128), F32),
            pltpu.VMEM((2, 2 * PAIRS, 512), BF16),
            pltpu.VMEM((steps, 2, 2, PAIRS, width), BF16),
            pltpu.SemaphoreType.DMA((steps, 2)),
        ],
        compiler_params=vmem(56),
        name="inverse",
    )(in_vmem(y), table)
    return out.reshape(16, 4, 128, 128)


def update_kernel(se_ref, sp_ref, f_ref, old_ent, old_pres, oe_ref, op_ref):
    at = pl.ds(8 * pl.program_id(0), 8)
    oe_ref[...] = se_ref[...] + 0.5 * f_ref[0, at].astype(F32)
    op_ref[...] = sp_ref[...] + 0.5 * f_ref[1, at].astype(F32)


def update(start_entropy, start_pressure, filtered, ent, pres):
    whole = pl.BlockSpec((8, ROWS, COLS), lambda g: (g, 0, 0))
    anywhere = pl.BlockSpec(memory_space=pl.ANY)
    return pl.pallas_call(
        update_kernel,
        grid=(FLEV // 8,),
        in_specs=[whole, whole, IN_VMEM, anywhere, anywhere],
        out_specs=[whole, whole],
        out_shape=[pltpu.HBM((LEV, ROWS, COLS), F32)] * 2,
        input_output_aliases={3: 0, 4: 1},
        compiler_params=vmem(56),
        name="update",
    )(start_entropy, start_pressure, in_vmem(filtered), ent, pres)


def per_device(entropy, zonal_flux, meridional_flux, start_entropy, start_pressure, order_slot):
    n_lat = lax.axis_size("lat")
    n_lon = lax.axis_size("lonr")
    pairs = order_slot.reshape(PAIRS, 2)
    first_even = (pairs[:, 0] % 2) == 0
    even = jnp.where(first_even, pairs[:, 0], pairs[:, 1])
    odd = jnp.where(first_even, pairs[:, 1], pairs[:, 0])
    block = lax.axis_index("lat") * n_lon + lax.axis_index("lonr")
    both = jnp.stack((even, odd), axis=1)
    orders = lax.dynamic_slice_in_dim(both, block * 3, 3).reshape(6)
    swap = jnp.where(first_even, 0, 1).astype(jnp.int32)
    swap = lax.dynamic_slice_in_dim(swap, block * 3, 3)
    base = 2 * jnp.arange(3, dtype=jnp.int32)
    slots = jnp.stack((base + swap, base + 1 - swap), axis=1).reshape(6)

    first = (lax.axis_index("lat") * ROWS).astype(jnp.int32).reshape(1)
    side, south, north, fs, rc = edges(first, entropy, zonal_flux, meridional_flux)
    ring = range(n_lon)
    from_west = lax.ppermute(side, "lonr", [(i, (i + 1) % n_lon) for i in ring])
    from_east = lax.ppermute(side, "lonr", [((i + 1) % n_lon, i) for i in ring])
    from_north = lax.ppermute(south, "lat", [(i, i + 1) for i in range(n_lat - 1)])
    from_south = lax.ppermute(north, "lat", [(i + 1, i) for i in range(n_lat - 1)])
    table = fourier_table(jnp.stack((even, odd)))
    fields = (entropy, zonal_flux, meridional_flux)
    halos = (from_west, from_east, side, from_north, from_south)

    def exchange(items):
        return lax.all_to_all(
            items.reshape(16, 2, ROWS, COLS), "lonr", split_axis=0, concat_axis=0, tiled=True
        )

    first_items = exchange(tendencies(fields, halos, (fs, rc), half=0))
    later, *inputs = lax.optimization_barrier(
        [tendencies(fields, halos, (fs, rc), half=1), *legendre_inputs(orders), slots]
    )
    slots = inputs.pop()
    second_items = exchange(later)
    ent, pres = tendencies(fields, halos, (fs, rc), starts=[start_entropy, start_pressure])
    rows = forward(first_items, table)
    spectral = forward(second_items, table, rows)
    analysis, synthesis = legendre_tables(inputs)
    spectral = lax.all_to_all(
        spectral, ("lat", "lonr"), split_axis=0, concat_axis=0, tiled=True
    )
    spectrum, back = legendre_filter(
        spectral.reshape(8, 16, 6, 8, 128), analysis, synthesis, orders, slots
    )
    back = lax.all_to_all(
        back.reshape(128, 48, 128), ("lat", "lonr"), split_axis=0, concat_axis=0, tiled=True
    )
    filtered = inverse(back, table)
    filtered = lax.all_to_all(filtered, "lonr", split_axis=0, concat_axis=0, tiled=True)
    new_entropy, new_pressure = update(
        start_entropy, start_pressure, filtered.reshape(2, FLEV, ROWS, COLS), ent, pres
    )
    return new_entropy, new_pressure, spectrum.reshape(6, 64, 2, ORDERS)


def solution(mesh):
    cube = P(None, "lat", "lonr")
    return jax.shard_map(
        per_device,
        mesh=mesh,
        in_specs=(cube, cube, cube, cube, cube, P()),
        out_specs=(cube, cube, P(("lat", "lonr"), None, None, None)),
        check_vma=False,
    )
```

```python
import functools
import math

import jax
import jax.numpy as jnp
from jax import lax
from jax.experimental import pallas as pl
from jax.experimental.pallas import tpu as pltpu
import numpy as np
from jax.sharding import PartitionSpec as P

FLEV = 32
LEV = 40
NLAT = 1024
NLON = 2048
ORDERS = 768
PAIRS = ORDERS // 2
ROWS = 128
COLS = 128
F32 = jnp.float32
BF16 = jnp.bfloat16

gamma_three_halves = 0.5 * math.log(math.pi) - math.log(2.0)


def vmem(mib):
    return pltpu.CompilerParams(vmem_limit_bytes=mib << 20)


IN_VMEM = pl.BlockSpec(memory_space=pltpu.VMEM)


def in_vmem(x):
    return pltpu.with_memory_space_constraint(x, pltpu.VMEM)


def lane_ids(shape):
    return lax.broadcasted_iota(jnp.int32, shape, len(shape) - 1)


def sine_of(n):
    x = jnp.minimum(n, NLAT - n) * (math.pi / NLAT)
    square = x * x
    total = jnp.full_like(x, 1.0 / math.factorial(13))
    for power in (11, 9, 7, 5, 3, 1):
        total = total * square + (-1.0) ** (power // 2) / math.factorial(power)
    return total * x


def edges_kernel(
    first_ref, s_any, u_any, v_ref, side_ref, south_ref, north_ref, fs_ref, rc_ref,
    s_ref, u_ref, sems
):
    lane = lane_ids((8, 128))
    owner = ((lane + 3) & 127) >> 3
    part = lane & 7
    parts = LEV // 8

    def fetch(n, g):
        at = pl.ds(8 * g, 8)
        src = (s_any, u_any)[n]
        dst = (s_ref, u_ref)[n]
        return pltpu.make_async_copy(src.at[at], dst.at[at], sems.at[n, g])

    for g in range(parts):
        for n in range(2):
            fetch(n, g).start()
    at = first_ref[0] - 8 + lax.broadcasted_iota(jnp.int32, (136, 128), 0)
    sines = sine_of((at + 1).astype(F32))
    fs_ref[...] = jnp.where((at >= 0) & (at < NLAT - 1), sines, 0.0)
    rc_ref[...] = 1.0 / sine_of(at[8:].astype(F32) + 0.5)

    def four_levels(q, carry):
        for k in range(4):
            lev = 4 * q + k
            side = jnp.zeros((8, 128), F32)
            flux = jnp.zeros((8, 128), F32)
            for i in range(16):
                s = s_ref[lev, pl.ds(8 * i, 8), :]
                u = u_ref[lev, pl.ds(8 * i, 8), :]
                side = jnp.where(owner == i, pltpu.roll(s, 8 * i, 1) if i else s, side)
                flux = jnp.where(owner == i, pltpu.roll(u, 8 * i, 1) if i else u, flux)
            side_ref[lev] = jnp.where(part == 4, pltpu.roll(flux, 125, 1), side)
            south_ref[lev, 0:3, :] = s_ref[lev, 125:128, :]
            north_ref[lev] = s_ref[lev, 0:4, :]
        return carry

    for g in range(parts):
        for n in range(2):
            fetch(n, g).wait()
        lax.fori_loop(2 * g, 2 * g + 2, four_levels, 0)
    for lev in range(LEV):
        south_ref[lev, 3:4, :] = v_ref[lev, 7:8, :]


def edges(first, entropy, zonal, merid):
    anywhere = pl.BlockSpec(memory_space=pl.ANY)
    return pl.pallas_call(
        edges_kernel,
        grid=(1,),
        in_specs=[pl.BlockSpec(memory_space=pltpu.SMEM), anywhere, anywhere, pl.BlockSpec((LEV, 8, COLS), lambda g: (0, ROWS // 8 - 1, 0))],
        out_specs=[pl.BlockSpec((LEV, n, 128), lambda g: (0, 0, 0)) for n in (8, 4, 4)]
        + [pl.BlockSpec((n, 128), lambda g: (0, 0)) for n in (136, 128)],
        out_shape=[
            pltpu.HBM((LEV, 8, 128), F32),
            pltpu.HBM((LEV, 4, 128), F32),
            pltpu.HBM((LEV, 4, 128), F32),
            pltpu.HBM((136, 128), F32),
            pltpu.HBM((128, 128), F32),
        ],
        scratch_shapes=[pltpu.VMEM((LEV, ROWS, COLS), F32)] * 2
        + [pltpu.SemaphoreType.DMA((2, LEV // 8))],
        name="edges",
    )(first, entropy, zonal, merid)


def stencil(x0, x1, x2, x3, x4, x5):
    return (37.0 * (x2 + x3) - 8.0 * (x1 + x4) + (x0 + x5)) * (1.0 / 60.0)


def stencil_matrices():
    weights = {-2: 1.0, -1: -8.0, 0: 37.0, 1: 37.0, 2: -8.0, 3: 1.0}
    along = np.zeros((256, 256), np.float32)
    across = np.zeros((128, 136), np.float32)
    for face in range(128):
        for shift, weight in weights.items():
            cell = face + shift
            along[cell if 0 <= cell < 128 else 128 + cell % 128 if cell >= 128 else 256 + cell, face] = weight
            across[face, cell if 0 <= cell < 128 else 128 + 4 + cell % 128 if cell >= 128 else 128 + 3 + cell] = weight
    along[128 + 3, 128 + 127] = 1.0
    along[128 + 124, 128] = 1.0
    return along, across


def split(x):
    high = x.astype(BF16)
    return high, (x - high.astype(F32)).astype(BF16)


def tend_kernel(*refs):
    (s_ref, u_ref, v_ref, hw_ref, he_ref, ow_ref, hn_ref, hs_ref, fs_ref, rc_ref, along_ref,
     across_ref) = refs[:12]
    cells, face, mext = refs[-3:]
    wide = s_ref.shape[1]
    lane = lane_ids((ROWS, COLS))
    small = lane_ids((8, 128)) & 7
    across = across_ref[...]

    def prepare(lev):
        west = hw_ref[lev // wide, lev % wide]
        own = ow_ref[lev // wide, lev % wide]
        edge = stencil(
            pltpu.roll(west, 6, 1), pltpu.roll(west, 5, 1), pltpu.roll(west, 4, 1),
            pltpu.roll(own, 3, 1), pltpu.roll(own, 2, 1), pltpu.roll(own, 1, 1),
        )
        edge = edge * pltpu.roll(west, 7, 1)
        rim = jnp.where(small < 3, he_ref[lev // wide, lev % wide], jnp.where(small == 3, edge, west))
        rim = jnp.concatenate([pltpu.roll(rim, (128 - 8 * i) % 128, 1) for i in range(16)])
        s = s_ref[lev // wide, lev % wide]
        s_hi, s_lo = split(s)
        r_hi, r_lo = split(rim)
        at = slice(128 * lev, 128 * lev + 128)
        cells[at, 0:128] = s_hi
        cells[at, 128:256] = r_hi
        cells[at, 256:384] = s_lo
        cells[at, 384:512] = r_lo
        h_hi, h_lo = split(jnp.concatenate([hn_ref[lev // wide, lev % wide], hs_ref[lev // wide, lev % wide]]))
        face[lev, :, 256:384] = jnp.dot(
            across, jnp.concatenate([s_hi, s_lo, h_hi, h_lo]), preferred_element_type=F32
        )

    def multiply(part):
        rows = slice(512 * part, 512 * part + 512)
        res = jnp.dot(cells[rows, :], along_ref[...], preferred_element_type=F32)
        face[4 * part:4 * part + 4, :, 0:256] = res.reshape(4, 128, 256)

    def level(lev):
        half = lev % 4
        u = u_ref[lev // wide, lev % wide]
        z = (u * (1.0 / 60.0)) * face[lev, :, 0:128]
        rim = face[lev, :, 128:256]
        dz = z - pltpu.roll(jnp.where(lane == COLS - 1, rim, z), 1, 1)
        du = u - jnp.where(lane == 0, rim, pltpu.roll(u, 1, 1))
        fv = v_ref[lev // wide, lev % wide] * fs_ref[8:136, :]
        fv_top = hn_ref[lev // wide, lev % wide, 3:4, :] * fs_ref[7:8, :]
        top = [hn_ref[lev // wide, lev % wide, o:o + 1, :] for o in range(3)] + [s_ref[lev // wide, lev % wide, o:o + 1, :] for o in range(3)]
        m = fv * (face[lev, :, 256:384] * (1.0 / 60.0))
        mext[half, 0, 7:8, :] = fv_top * stencil(*top)
        mext[half, 0, 8:136, :] = m
        mext[half, 1, 7:8, :] = fv_top
        mext[half, 1, 8:136, :] = fv
        rc = rc_ref[...]
        ent = -(dz + (m - mext[half, 0, 7:135, :]) * rc)
        pres = -0.3 * (du + (fv - mext[half, 1, 7:135, :]) * rc)
        return ent, pres

    def put(lev, ent, pres):
        if len(refs) == 16:
            item_ref = refs[12]
            item_ref[0, lev // 2, lev % 2] = ent.astype(BF16)
            item_ref[1, lev // 2, lev % 2] = pres.astype(BF16)
        else:
            se_ref, sp_ref, ent_ref, pres_ref = refs[12:16]
            ent_ref[lev] = se_ref[lev] + 0.5 * ent
            pres_ref[lev] = sp_ref[lev] + 0.5 * pres

    for lev in range(4):
        prepare(lev)
    multiply(0)
    for lev in range(4, 8):
        prepare(lev)
    multiply(1)
    for lev in range(8):
        put(lev, *level(lev))


def tendencies(fields, halos, factors, starts=None, half=None):
    groups = LEV // 4
    if half is None:
        deep, wide, steps = 2, 4, 1

        def at(g):
            return (FLEV // 8, 0)
    else:
        deep, wide, steps = 4, 2, 2

        def at(g):
            return (g, half)

    def spec(rows):
        return pl.BlockSpec((deep, wide, rows, 128), lambda g: at(g) + (0, 0))

    along, across = stencil_matrices()
    along = jnp.asarray(np.concatenate((along, along)), BF16)
    across = np.concatenate(
        (across[:, :128], across[:, :128], across[:, 128:], across[:, 128:]), axis=1
    )
    operands = [x.reshape(groups, 4, *x.shape[1:]) for x in (*fields, *halos)]
    in_specs = [spec(x.shape[2]) for x in operands]
    operands += [*factors, along, jnp.asarray(across, BF16)]
    in_specs += [
        pl.BlockSpec((136, 128), lambda g: (0, 0)),
        pl.BlockSpec((128, 128), lambda g: (0, 0)),
        pl.BlockSpec((512, 256), lambda g: (0, 0)),
        pl.BlockSpec((128, 272), lambda g: (0, 0)),
    ]
    if half is None:
        tail = pl.BlockSpec((8, ROWS, COLS), lambda g: (FLEV // 8, 0, 0))
        operands += starts
        in_specs += [tail, tail]
        out_specs = [tail, tail]
        out_shape = [pltpu.HBM((LEV, ROWS, COLS), F32)] * 2
    else:
        out_specs = pl.BlockSpec((2, 4, 2, ROWS, COLS), lambda g: (0, g, 0, 0, 0))
        out_shape = pltpu.HBM((2, 8, 2, ROWS, COLS), BF16)
    return pl.pallas_call(
        tend_kernel,
        grid=(steps,),
        in_specs=in_specs,
        out_specs=out_specs,
        out_shape=out_shape,
        scratch_shapes=[
            pltpu.VMEM((1024, 512), BF16),
            pltpu.VMEM((8, 128, 384), F32),
            pltpu.VMEM((4, 2, 136, 128), F32),
        ],
        name="tendencies" if half is not None else "tail",
    )(*operands)


def table_kernel(base_ref, turn_ref, out_ref):
    for par in range(2):
        c = base_ref[par, 0]
        s = base_ref[par, 1]
        for b in range(8):
            tc = jnp.broadcast_to(turn_ref[par, :, b:b + 1], c.shape)
            ts = jnp.broadcast_to(turn_ref[par, :, 8 + b:9 + b], c.shape)
            out_ref[par, 0, :, 128 * b:128 * b + 128] = (c * tc - s * ts).astype(BF16)
            out_ref[par, 1, :, 128 * b:128 * b + 128] = (s * tc + c * ts).astype(BF16)


def fourier_table(even_odd):
    def angles(steps):
        product = (even_odd[:, :, None] * steps[None, None, :]) % NLON
        return (2.0 * math.pi / NLON) * product.astype(F32)

    near = angles(jnp.arange(128, dtype=jnp.int32))
    far = angles(128 * jnp.arange(8, dtype=jnp.int32))
    base = jnp.stack((jnp.cos(near), jnp.sin(near)), axis=1)
    turn = jnp.concatenate((jnp.cos(far), jnp.sin(far)), axis=2)
    tile = 96
    return pl.pallas_call(
        table_kernel,
        grid=(PAIRS // tile,),
        in_specs=[
            pl.BlockSpec((2, 2, tile, 128), lambda g: (0, 0, g, 0)),
            pl.BlockSpec((2, tile, 16), lambda g: (0, g, 0)),
        ],
        out_specs=pl.BlockSpec((2, 2, tile, NLON // 2), lambda g: (0, 0, g, 0)),
        out_shape=pltpu.HBM((2, 2, PAIRS, NLON // 2), BF16),
        name="longitude_table",
    )(base, turn)


def forward_kernel(half, *refs):
    if half == 0:
        x_ref, t_any, rows, fold, t_ref, sems = refs
    else:
        x_ref, t_any, r_any, o_ref, fold, t_ref, sems, rows = refs
    par = pl.program_id(0)

    def fetch(n):
        return pltpu.make_async_copy(t_any.at[n], t_ref.at[n], sems.at[n])

    @pl.when(par == 0)
    def _():
        fetch(0).start()
        if half:
            pltpu.make_async_copy(r_any, rows, sems.at[2]).start()
        fetch(1).start()

    for a in range(2):
        for b in range(8):
            lo = x_ref[b, a]
            hi = x_ref[b + 8, a]
            fold[128 * a:128 * a + 128, 128 * b:128 * b + 128] = lo + jnp.where(par == 0, hi, -hi)
    fetch(par).wait()
    res = lax.dot_general(
        t_ref[par].reshape(2 * PAIRS, NLON // 2), fold[...], (((1,), (1,)), ((), ())),
        preferred_element_type=F32,
    )
    if half:
        @pl.when(par == 0)
        def _():
            pltpu.make_async_copy(r_any, rows, sems.at[2]).wait()

    for ri in range(2):
        for a in range(2):
            rows[pl.ds(8 * par + 2 * (2 * half + a) + ri, PAIRS, stride=16), :] = (
                res[PAIRS * ri:PAIRS * ri + PAIRS, 128 * a:128 * a + 128]
            )

    if half:
        @pl.when(par == 1)
        def _():
            o_ref[...] = rows[...].reshape(o_ref.shape).astype(BF16)


def forward(x, table, rows=None):
    half = 0 if rows is None else 1
    anywhere = pl.BlockSpec(memory_space=pl.ANY)
    buffers = [
        pltpu.VMEM((256, NLON // 2), BF16),
        pltpu.VMEM((2, 2, PAIRS, NLON // 2), BF16),
        pltpu.SemaphoreType.DMA((3,)),
    ]
    if half == 0:
        operands = [in_vmem(x), table]
        out_specs = pl.BlockSpec((16 * PAIRS, 128), lambda g: (0, 0))
        out_shape = pltpu.HBM((16 * PAIRS, 128), F32)
    else:
        operands = [in_vmem(x), table, rows]
        out_specs = pl.BlockSpec((128, 48, 128), lambda g: (0, 0, 0))
        out_shape = pltpu.HBM((128, 48, 128), BF16)
        buffers.append(pltpu.VMEM((16 * PAIRS, 128), F32))
    return pl.pallas_call(
        functools.partial(forward_kernel, half),
        grid=(2,),
        in_specs=[IN_VMEM] + [anywhere] * (len(operands) - 1),
        out_specs=out_specs,
        out_shape=out_shape,
        scratch_shapes=buffers,
        compiler_params=vmem(56),
        name="forward",
    )(*operands)


CHUNK = 128


def legendre_kernel(a_ref, b_ref, m_ref, cos_ref, start_ref, w_ref, ana_ref, syn_ref, rows, state):
    chunk = pl.program_id(0)
    upper = lax.broadcasted_iota(jnp.int32, (8, 128), 0) < 4

    @pl.when(chunk == 0)
    def _():
        state[...] = jnp.zeros_like(state)

    cosine = [cos_ref[8 * v:8 * v + 8, :] for v in range(3)]
    orders = [m_ref[8 * v:8 * v + 8, :] for v in range(3)]

    def body(it, carry):
        prev, curr, logs, scale = carry
        for k in range(4):
            local = it * 4 + k
            degree = chunk * CHUNK + local
            nxt = []
            new_logs = []
            new_scale = []
            for v in range(3):
                at = degree * 6 + 2 * v
                a = jnp.where(upper, a_ref[at], a_ref[at + 1])
                b = jnp.where(upper, b_ref[at], b_ref[at + 1])
                first = orders[v] == degree
                start = start_ref[8 * v:8 * v + 8, :]
                val = jnp.where(first, 1.0, (a * cosine[v]) * curr[v] - b * prev[v])
                lg = jnp.where(first, start, logs[v])
                sc = jnp.where(first, start_ref[24 + 8 * v:32 + 8 * v, :], scale[v])
                row = pl.multiple_of(local * 24, 8) + 8 * v
                rows[pl.ds(row, 8), :] = val * sc
                nxt.append(val)
                new_logs.append(lg)
                new_scale.append(sc)
            prev, curr, logs, scale = curr, nxt, new_logs, new_scale
        grow = [jnp.maximum(1.0, jnp.maximum(jnp.abs(p), jnp.abs(c))) for p, c in zip(prev, curr)]
        inv = [1.0 / g for g in grow]
        prev = [p * i for p, i in zip(prev, inv)]
        curr = [c * i for c, i in zip(curr, inv)]
        logs = [l + jnp.log(g) for l, g in zip(logs, grow)]
        scale = [jnp.where(s > -1.0, jnp.where(o <= chunk * CHUNK + it * 4 + 3, jnp.exp(l), 0.0), 0.0)
                 for s, l, o in zip(scale, logs, orders)]
        return prev, curr, logs, scale

    init = tuple([state[24 * n + 8 * v:24 * n + 8 * v + 8, :] for v in range(3)] for n in range(4))
    final = lax.fori_loop(0, CHUNK // 4, body, init)
    for n in range(4):
        for v in range(3):
            state[24 * n + 8 * v:24 * n + 8 * v + 8, :] = final[n][v]
    for o in range(6):
        for jb in range(4):
            val = rows[pl.ds(4 * o + jb, CHUNK, stride=24), :]
            syn_ref[o, :, 128 * jb:128 * jb + 128] = val.astype(BF16)
            ana_ref[o, :, 128 * jb:128 * jb + 128] = (val * w_ref[jb:jb + 1, :]).astype(BF16)


def legendre_inputs(orders):
    half = NLAT // 2
    colatitude = math.pi * (jnp.arange(half, dtype=F32) + 0.5) / NLAT
    sine = jnp.sin(colatitude)
    order_f = orders.astype(F32)
    log_start = (
        -0.5 * math.log(2.0)
        + 0.5 * (lax.lgamma(order_f + 1.5) - gamma_three_halves - lax.lgamma(order_f + 1.0))
    )[:, None] + order_f[:, None] * jnp.log(sine)[None, :]
    log_start = log_start.reshape(24, 128)
    start = jnp.concatenate((log_start, jnp.exp(log_start)))
    cosine = jnp.tile(jnp.cos(colatitude).reshape(4, 128), (6, 1))
    weight = (sine * (math.pi / NLAT)).reshape(4, 128)
    deg = jnp.arange(ORDERS, dtype=F32)[:, None]
    running = orders[None, :] < jnp.arange(ORDERS, dtype=jnp.int32)[:, None]
    denom_a = jnp.maximum(deg * deg - order_f * order_f, 1.0)
    coef_a = jnp.where(running, jnp.sqrt(jnp.maximum(4.0 * deg * deg - 1.0, 0.0) / denom_a), 0.0)
    numer_b = jnp.maximum((deg - 1.0) * (deg - 1.0) - order_f * order_f, 0.0)
    denom_b = jnp.maximum(4.0 * (deg - 1.0) * (deg - 1.0) - 1.0, 1.0)
    coef_b = coef_a * jnp.sqrt(numer_b / denom_b)
    order_rows = jnp.broadcast_to(jnp.repeat(orders, 4)[:, None], (24, 128))
    return [coef_a.reshape(-1), coef_b.reshape(-1), order_rows, cosine, start, weight]


def legendre_tables(inputs):
    half = NLAT // 2
    smem = pl.BlockSpec(memory_space=pltpu.SMEM)
    full = pl.BlockSpec((24, 128), lambda g: (0, 0))
    return pl.pallas_call(
        legendre_kernel,
        grid=(ORDERS // CHUNK,),
        in_specs=[
            smem, smem, full, full,
            pl.BlockSpec((48, 128), lambda g: (0, 0)),
            pl.BlockSpec((4, 128), lambda g: (0, 0)),
        ],
        out_specs=[pl.BlockSpec((6, CHUNK, half), lambda g: (0, g, 0))] * 2,
        out_shape=[pltpu.HBM((6, ORDERS, half), BF16)] * 2,
        scratch_shapes=[pltpu.VMEM((CHUNK * 24, 128), F32), pltpu.VMEM((96, 128), F32)],
        name="legendre_tables",
    )(*inputs)


def filter_kernel(
    slot_ref, ord_ref, f_ref, ana_high, ana_full, syn_high, syn_full, spec_ref, back_ref
):
    sub = lax.broadcasted_iota(jnp.int32, (128, 128), 0)
    flip = jnp.where(sub + lane_ids((128, 128)) == 127, 1.0, 0.0).astype(BF16)
    pair = pl.program_id(0)
    above = (ord_ref[2 * pair] < ORDERS // 2).astype(jnp.int32)
    for k, low, ana_ref, syn_ref in (
        (above, ORDERS // 2, ana_high, syn_high), (1 - above, 0, ana_full, syn_full)
    ):
        width = ORDERS - low
        o = 2 * pair + k
        order = ord_ref[o]
        plus = []
        minus = []
        for c in range(4):
            north = f_ref[c, :, o].astype(F32).reshape(128, 128)
            south = f_ref[7 - c, :, o].astype(F32).reshape(128, 128).astype(BF16)
            south = jnp.dot(south, flip, preferred_element_type=F32)
            plus.append((north + south).astype(BF16))
            minus.append((north - south).astype(BF16))
        both = jnp.concatenate(
            [jnp.concatenate(plus, axis=1), jnp.concatenate(minus, axis=1)], axis=0
        )
        coef = lax.dot_general(
            both, ana_ref[0], (((1,), (1,)), ((), ())), preferred_element_type=F32
        )
        even = ((lane_ids((128, width)) - order) & 1) == 0
        spec = jnp.where(even, coef[:128], coef[128:])
        if low:
            spec_ref[slot_ref[o] & 1, :, :low] = jnp.zeros((128, low), F32)
        spec_ref[slot_ref[o] & 1, :, low:] = spec
        parts = jnp.concatenate([jnp.where(even, spec, 0.0), jnp.where(even, 0.0, spec)], axis=0)
        grid = jnp.dot(parts.astype(BF16), syn_ref[0], preferred_element_type=F32)
        factor = jnp.where(order == 0, 0.5, 1.0)
        north = (grid[:128] + grid[128:]) * factor
        south = ((grid[:128] - grid[128:]) * factor).astype(BF16)
        for c in range(4):
            cut = slice(128 * c, 128 * c + 128)
            back_ref[c, :, k] = north[:, cut].reshape(16, 8, 128).astype(BF16)
            turned = jnp.dot(south[:, cut], flip, preferred_element_type=F32)
            back_ref[7 - c, :, k] = turned.reshape(16, 8, 128).astype(BF16)


def legendre_filter(fourier, analysis, synthesis, orders, slots):
    def above(p, order):
        return (order[2 * p] < ORDERS // 2).astype(jnp.int32)

    high = pl.BlockSpec(
        (1, ORDERS // 2, NLAT // 2), lambda p, slot, order: (2 * p + above(p, order), 1, 0)
    )
    full = pl.BlockSpec(
        (1, ORDERS, NLAT // 2), lambda p, slot, order: (2 * p + 1 - above(p, order), 0, 0)
    )
    blocks = pl.BlockSpec((8, 16, 2, 8, 128), lambda p, *_: (0, 0, p, 0, 0))
    return pl.pallas_call(
        filter_kernel,
        grid_spec=pltpu.PrefetchScalarGridSpec(
            num_scalar_prefetch=2,
            grid=(3,),
            in_specs=[IN_VMEM, high, full, high, full],
            out_specs=[
                pl.BlockSpec((2, 128, ORDERS), lambda p, *_: (p, 0, 0)),
                blocks,
            ],
        ),
        out_shape=[
            pltpu.HBM((6, 128, ORDERS), F32),
            pltpu.HBM((8, 16, 6, 8, 128), BF16),
        ],
        compiler_params=vmem(56),
        name="legendre_filter",
    )(slots, orders, in_vmem(fourier), analysis, analysis, synthesis, synthesis)


def inverse_kernel(y_ref, t_any, o_ref, rows, cols, t_ref, sems):
    step = pl.program_id(0)
    width = NLON // 2 // 2

    def fetch(n, par):
        at = pl.ds(pl.multiple_of(n * width, width), width)
        return pltpu.make_async_copy(
            t_any.at[par, :, :, at], t_ref.at[n, par], sems.at[n, par]
        )

    @pl.when(step == 0)
    def _():
        for n in range(2):
            for par in range(2):
                fetch(n, par).start()
        rows[...] = y_ref[...].astype(F32).reshape(rows.shape)
        for par in range(2):
            for ri in range(2):
                for a in range(4):
                    cols[par, PAIRS * ri:PAIRS * ri + PAIRS, 128 * a:128 * a + 128] = (
                        rows[pl.ds(8 * par + 2 * a + ri, PAIRS, stride=16), :].astype(BF16)
                    )

    sums = []
    for par in range(2):
        fetch(step, par).wait()
        res = lax.dot_general(
            cols[par], t_ref[step, par].reshape(2 * PAIRS, width), (((0,), (0,)), ((), ())),
            preferred_element_type=F32,
        )
        sums.append(res * (2.0 / NLON))
    low = (sums[0] + sums[1]).astype(BF16)
    high = (sums[0] - sums[1]).astype(BF16)
    for b in range(width // 128):
        o_ref[0, b] = low[:, 128 * b:128 * b + 128].reshape(4, 128, 128)
        o_ref[1, b] = high[:, 128 * b:128 * b + 128].reshape(4, 128, 128)


def inverse(y, table):
    steps = 2
    width = NLON // 2 // steps
    out = pl.pallas_call(
        inverse_kernel,
        grid=(steps,),
        in_specs=[
            IN_VMEM,
            pl.BlockSpec(memory_space=pl.ANY),
        ],
        out_specs=pl.BlockSpec((2, width // 128, 4, 128, 128), lambda g: (0, g, 0, 0, 0)),
        out_shape=pltpu.HBM((2, 8, 4, 128, 128), BF16),
        scratch_shapes=[
            pltpu.VMEM((128 * 48, 128), F32),
            pltpu.VMEM((2, 2 * PAIRS, 512), BF16),
            pltpu.VMEM((steps, 2, 2, PAIRS, width), BF16),
            pltpu.SemaphoreType.DMA((steps, 2)),
        ],
        compiler_params=vmem(56),
        name="inverse",
    )(in_vmem(y), table)
    return out.reshape(16, 4, 128, 128)


def update_kernel(se_ref, sp_ref, f_ref, old_ent, old_pres, oe_ref, op_ref):
    at = pl.ds(8 * pl.program_id(0), 8)
    oe_ref[...] = se_ref[...] + 0.5 * f_ref[0, at].astype(F32)
    op_ref[...] = sp_ref[...] + 0.5 * f_ref[1, at].astype(F32)


def update(start_entropy, start_pressure, filtered, ent, pres):
    whole = pl.BlockSpec((8, ROWS, COLS), lambda g: (g, 0, 0))
    anywhere = pl.BlockSpec(memory_space=pl.ANY)
    return pl.pallas_call(
        update_kernel,
        grid=(FLEV // 8,),
        in_specs=[whole, whole, IN_VMEM, anywhere, anywhere],
        out_specs=[whole, whole],
        out_shape=[pltpu.HBM((LEV, ROWS, COLS), F32)] * 2,
        input_output_aliases={3: 0, 4: 1},
        compiler_params=vmem(56),
        name="update",
    )(start_entropy, start_pressure, in_vmem(filtered), ent, pres)


def per_device(entropy, zonal_flux, meridional_flux, start_entropy, start_pressure, order_slot):
    n_lat = lax.axis_size("lat")
    n_lon = lax.axis_size("lonr")
    pairs = order_slot.reshape(PAIRS, 2)
    first_even = (pairs[:, 0] % 2) == 0
    even = jnp.where(first_even, pairs[:, 0], pairs[:, 1])
    odd = jnp.where(first_even, pairs[:, 1], pairs[:, 0])
    block = lax.axis_index("lat") * n_lon + lax.axis_index("lonr")
    both = jnp.stack((even, odd), axis=1)
    orders = lax.dynamic_slice_in_dim(both, block * 3, 3).reshape(6)
    swap = jnp.where(first_even, 0, 1).astype(jnp.int32)
    swap = lax.dynamic_slice_in_dim(swap, block * 3, 3)
    base = 2 * jnp.arange(3, dtype=jnp.int32)
    slots = jnp.stack((base + swap, base + 1 - swap), axis=1).reshape(6)

    first = (lax.axis_index("lat") * ROWS).astype(jnp.int32).reshape(1)
    side, south, north, fs, rc = edges(first, entropy, zonal_flux, meridional_flux)
    ring = range(n_lon)
    from_west = lax.ppermute(side, "lonr", [(i, (i + 1) % n_lon) for i in ring])
    from_east = lax.ppermute(side, "lonr", [((i + 1) % n_lon, i) for i in ring])
    from_north = lax.ppermute(south, "lat", [(i, i + 1) for i in range(n_lat - 1)])
    from_south = lax.ppermute(north, "lat", [(i + 1, i) for i in range(n_lat - 1)])
    table = fourier_table(jnp.stack((even, odd)))
    fields = (entropy, zonal_flux, meridional_flux)
    halos = (from_west, from_east, side, from_north, from_south)

    def exchange(items):
        return lax.all_to_all(
            items.reshape(16, 2, ROWS, COLS), "lonr", split_axis=0, concat_axis=0, tiled=True
        )

    first_items = exchange(tendencies(fields, halos, (fs, rc), half=0))
    later, *inputs = lax.optimization_barrier(
        [tendencies(fields, halos, (fs, rc), half=1), *legendre_inputs(orders), slots]
    )
    slots = inputs.pop()
    second_items = exchange(later)
    ent, pres = tendencies(fields, halos, (fs, rc), starts=[start_entropy, start_pressure])
    rows = forward(first_items, table)
    spectral = forward(second_items, table, rows)
    analysis, synthesis = legendre_tables(inputs)
    spectral = lax.all_to_all(
        spectral, ("lat", "lonr"), split_axis=0, concat_axis=0, tiled=True
    )
    spectrum, back = legendre_filter(
        spectral.reshape(8, 16, 6, 8, 128), analysis, synthesis, orders, slots
    )
    back = lax.all_to_all(
        back.reshape(128, 48, 128), ("lat", "lonr"), split_axis=0, concat_axis=0, tiled=True
    )
    filtered = inverse(back, table)
    filtered = lax.all_to_all(filtered, "lonr", split_axis=0, concat_axis=0, tiled=True)
    new_entropy, new_pressure = update(
        start_entropy, start_pressure, filtered.reshape(2, FLEV, ROWS, COLS), ent, pres
    )
    return new_entropy, new_pressure, spectrum.reshape(6, 64, 2, ORDERS)


def solution(mesh):
    cube = P(None, "lat", "lonr")
    return jax.shard_map(
        per_device,
        mesh=mesh,
        in_specs=(cube, cube, cube, cube, cube, P()),
        out_specs=(cube, cube, P(("lat", "lonr"), None, None, None)),
        check_vma=False,
    )
```
